256 devices in a mesh: gx: 16 (over y_hi, z), gy: 16 (over y_lo, x, core).
Axes of the slice: x: 4, y: 4 (y_hi: 2, y_lo: 2; y = y_hi * 2 + y_lo), z: 8, core: 2. Of those that a mesh axis runs over, the one named last changes fastest.
Arguments:
- state: float32 [8, 512, 2048], P(None, 'gx', 'gy'), may hold values from -6 to 6
- load_vector: bfloat16 [8, 512, 2048], P(None, 'gx', 'gy'), may hold values from -6 to 6
- active: int32 [512, 2048], P('gx', 'gy'), may hold values 0 or 1
- stiff_band: float32 [3, 5], replicated, may hold values from -0.6 to 1.2
- mass_band: float32 [3, 5], replicated, may hold values from 0.1 to 0.6
- eig_basis: float32 [3, 16, 16], replicated, may hold values from -1.5 to 1.5
- eig_values: float32 [3, 16], replicated, may hold values from 0.2 to 5
- cut_cols: int32 [16, 16, 2], P('gx', 'gy'), may hold values from -1 to 63, as said below
- cut_inverse: bfloat16 [16, 16, 2, 16, 256, 256], P('gx', 'gy'), may hold values from -0.375 to 0.375
Outputs:
- smoothed: float32 [8, 512, 2048], P(None, 'gx', 'gy')
The draws below stay inside these ranges and needn't reach their ends.
Inputs may be any that keep to these rules, and one draw needn't show every extreme that they name: `cut_cols`: on each device the entries that are not -1 name distinct local patch columns; a device holds 0 to 2 such entries and some device holds 2.
All inputs are finite; a program needn't handle non-finite values. No bound on the sum of `active` on one device may be relied on, other than what follows from the above.
Results may differ from the reference program's by a relative error of at most 0.0003.
Values sent between devices are 32-bit elements; how exact they have to be, the bound alone decides.
No kernel may reach another device: no remote copies, remote signals or barrier semaphores. Data moves between devices by JAX's collectives and lax.ppermute only.
A program may use at most 64 MiB of HBM per device.

```python
import math
import jax
import jax.numpy as jnp
from jax import lax

BAND = 4
PATCH = 16
CX = 32
CY = 128
NZ = 8
MOST = 2
COLS = 64
NX = 512
NY = 2048
N_GX = 16
N_GY = 16


def draw_cut_cols(key, part):
    tiles = N_GX * N_GY
    keys = jax.random.split(jax.random.fold_in(key, 11), tiles)
    orders = jax.vmap(lambda single: jax.random.permutation(single, COLS))(keys)[:, :MOST]
    counts = jax.random.randint(jax.random.fold_in(key, 12), (tiles,), 0, MOST + 1)
    chosen = jax.random.randint(jax.random.fold_in(key, 13), (), 0, tiles)
    counts = jnp.where(jnp.arange(tiles) == chosen, MOST, counts)
    in_use = jnp.arange(MOST)[None, :] < counts[:, None]
    return jnp.where(in_use, orders, -1).astype(jnp.int32).reshape(N_GX, N_GY, MOST)


def place_ends(array, own_key, smallest, top_value):
    dims = array.shape
    index_at = [jax.random.randint(jax.random.fold_in(own_key, axis), (), 0, dims[axis]) for axis in range(len(dims))]
    array = array.at[tuple(index_at)].set(smallest)
    longest = dims.index(max(dims))
    index_at[longest] = (index_at[longest] + 1) % dims[longest]
    return array.at[tuple(index_at)].set(top_value)


def shard_levels(key, dims, shards, low, high):
    def one(dim, shards_of):
        steps = jax.random.uniform(jax.random.fold_in(jax.random.fold_in(key, 6), dim), (shards_of,), jnp.float32, low / len(shards), high / len(shards))
        return jnp.repeat(jnp.exp(steps), dims[dim] // shards_of).reshape((-1,) + (1,) * (len(dims) - dim - 1))

    factor_of = one(*shards[0])
    for cut in shards[1:]:
        factor_of = factor_of * one(*cut)
    return factor_of


def normal_values(stream_key, shape, deviation, limit, shards=(), kind=jnp.bfloat16):
    values = deviation * jax.random.normal(stream_key, shape, jnp.float32)
    if shards:
        values = values * shard_levels(stream_key, shape, shards, -0.22, 0.18)
    return jnp.clip(values, -limit, limit).astype(kind)


def setup_inputs(seed: int = 0) -> dict:
    splits = jax.random.split(jax.random.key(seed), 10)
    return {
        "state": normal_values(splits[0], (NZ, NX, NY), 1.0, 6.0, ((1, 16), (2, 16)), jnp.float32),
        "load_vector": normal_values(splits[1], (NZ, NX, NY), 1.0, 6.0, ((1, 16), (2, 16))),
        "active": place_ends((jax.random.randint(splits[2], (NX, NY), 0, 4) < 3).astype(jnp.int32), jax.random.fold_in(splits[2], 1), 0, 1),
        "stiff_band": jnp.clip(jax.random.uniform(splits[3], (3, BAND + 1), jnp.float32, -0.6, 1.2), -0.6, 1.2),
        "mass_band": jnp.clip(jax.random.uniform(splits[4], (3, BAND + 1), jnp.float32, 0.1, 0.6), 0.1, 0.6),
        "eig_basis": normal_values(splits[5], (3, PATCH, PATCH), PATCH ** -0.5, 1.5, (), jnp.float32),
        "eig_values": jnp.clip(jnp.exp(jax.random.uniform(splits[6], (3, PATCH), jnp.float32, math.log(0.2), math.log(5.0))), 0.2, 5.0),
        "cut_cols": draw_cut_cols(jax.random.fold_in(splits[9], 71), 0),
        "cut_inverse": normal_values(splits[8], (N_GX, N_GY, MOST, PATCH, PATCH * PATCH, PATCH * PATCH), (PATCH * PATCH) ** -0.5, 0.375, ((0, 16), (1, 16))),
    }


damping = 0.5


def band_valid(values, coeffs, along):
    length = values.shape[along] - 2 * BAND
    result = coeffs[0] * lax.slice_in_dim(values, BAND, BAND + length, axis=along)
    for offset in range(1, BAND + 1):
        upper = lax.slice_in_dim(values, BAND + offset, BAND + offset + length, axis=along)
        lower = lax.slice_in_dim(values, BAND - offset, BAND - offset + length, axis=along)
        result = result + coeffs[offset] * (upper + lower)
    return result


def apply_operator(field, stiff_band, mass_band):
    padded = jnp.pad(field, ((BAND, BAND), (0, 0), (0, 0)))
    mass_z = band_valid(padded, mass_band[0], 0)
    stiff_z = band_valid(padded, stiff_band[0], 0)
    mass_xz = band_valid(mass_z, mass_band[1], 1)
    stiff_xz = band_valid(mass_z, stiff_band[1], 1)
    mass_x_stiff_z = band_valid(stiff_z, mass_band[1], 1)
    return band_valid(stiff_xz + mass_x_stiff_z, mass_band[2], 2) + band_valid(mass_xz, stiff_band[2], 2)


def fold_blocks(values, along, half_patch):
    lower = lax.slice_in_dim(values, 0, half_patch, axis=along + 1)
    upper = lax.slice_in_dim(values, half_patch, 2 * half_patch, axis=along + 1)
    widths_low = [(0, 0)] * values.ndim
    widths_high = [(0, 0)] * values.ndim
    widths_low[along] = (0, 1)
    widths_high[along] = (1, 0)
    return jnp.pad(lower, widths_low) + jnp.pad(upper, widths_high)


def reference(state, load_vector, active, stiff_band, mass_band, eig_basis, eig_values, cut_cols, cut_inverse):
    highest = lax.Precision.HIGHEST
    half_patch = PATCH // 2
    quarter = PATCH // 4
    blocks_x = NX // half_patch
    blocks_y = NY // half_patch
    blocks_z = NZ // half_patch
    local_x = CX // half_patch
    local_y = CY // half_patch
    live_mask = active.astype(jnp.float32)
    padded = jnp.pad(state, ((0, 0), (BAND, BAND), (BAND, BAND)))
    resid = live_mask[None] * (load_vector.astype(jnp.float32) - apply_operator(padded, stiff_band, mass_band))
    resid_pad = jnp.pad(resid, ((quarter, quarter), (quarter, quarter), (quarter, quarter)))
    basis_z, basis_x, basis_y = eig_basis[0], eig_basis[1], eig_basis[2]
    denom = 1.0 / (eig_values[0][:, None, None] + eig_values[1][None, :, None] + eig_values[2][None, None, :])
    tile_x = jnp.arange(N_GX, dtype=jnp.int32)[:, None, None]
    tile_y = jnp.arange(N_GY, dtype=jnp.int32)[None, :, None]
    column = jnp.maximum(cut_cols, 0)
    block_a = (tile_x * local_x + column // local_y).astype(jnp.int32)
    block_b = (tile_y * local_y + column % local_y).astype(jnp.int32)
    in_use = (cut_cols >= 0).astype(jnp.float32)
    colmask = jnp.zeros((blocks_x, blocks_y), jnp.float32).at[block_a.ravel(), block_b.ravel()].max(in_use.ravel())

    def add_row(block_row, accum):
        start = (block_row * half_patch).astype(jnp.int32)
        slab = lax.dynamic_slice_in_dim(resid_pad, start, PATCH, axis=1)
        blocks = slab.reshape(blocks_z + 1, half_patch, PATCH, blocks_y + 1, half_patch)
        blocks = jnp.concatenate([blocks[:-1], blocks[1:]], axis=1)
        blocks = jnp.concatenate([blocks[:, :, :, :-1], blocks[:, :, :, 1:]], axis=4)
        modes = jnp.einsum('zk,czxby->ckxby', basis_z, blocks, precision=highest)
        modes = jnp.einsum('xi,ckxby->ckiby', basis_x, modes, precision=highest)
        modes = jnp.einsum('yj,ckiby->ckibj', basis_y, modes, precision=highest)
        modes = modes * denom[None, :, :, None, :]
        modes = jnp.einsum('yj,ckibj->ckiby', basis_y, modes, precision=highest)
        modes = jnp.einsum('xi,ckiby->ckxby', basis_x, modes, precision=highest)
        back = jnp.einsum('zk,ckxby->czxby', basis_z, modes, precision=highest)
        keep = 1.0 - lax.dynamic_index_in_dim(colmask, block_row, 0, keepdims=False)
        back = back * keep[None, None, None, :, None]
        folded = fold_blocks(back, 3, half_patch).reshape(blocks_z, PATCH, PATCH, NY + half_patch)
        folded = fold_blocks(folded, 0, half_patch).reshape(NZ + half_patch, PATCH, NY + half_patch)
        current = lax.dynamic_slice_in_dim(accum, start, PATCH, axis=1)
        return lax.dynamic_update_slice_in_dim(accum, current + folded, start, axis=1)

    accum = jnp.zeros((NZ + half_patch, NX + half_patch, NY + half_patch), jnp.float32)
    accum = lax.fori_loop(0, blocks_x, add_row, accum)
    slots = N_GX * N_GY * MOST
    flat_cols = cut_cols.reshape(slots)
    flat_inverse = cut_inverse.reshape(slots, PATCH, PATCH * PATCH, PATCH * PATCH)

    def add_cut(slot_index, accum):
        entry = flat_cols[slot_index]
        in_use = (entry >= 0).astype(jnp.float32)
        entry = jnp.maximum(entry, 0)
        tile_row = slot_index // (N_GY * MOST)
        tile_col = (slot_index // MOST) % N_GY
        start_x = ((tile_row * local_x + entry // local_y) * half_patch).astype(jnp.int32)
        start_y = ((tile_col * local_y + entry % local_y) * half_patch).astype(jnp.int32)
        anchor = jnp.zeros((), jnp.int32)
        column_cells = lax.dynamic_slice(resid_pad, (anchor, start_x, start_y), (NZ + half_patch, PATCH, PATCH))
        blocks = column_cells.reshape(blocks_z + 1, half_patch, PATCH * PATCH)
        blocks = jnp.concatenate([blocks[:-1], blocks[1:]], axis=1)
        zmodes = jnp.einsum('zk,czq->ckq', basis_z, blocks, precision=highest)
        zmodes = lax.optimization_barrier(zmodes.astype(jnp.bfloat16)).astype(jnp.float32)
        inverse = lax.dynamic_index_in_dim(flat_inverse, slot_index, 0, keepdims=False).astype(jnp.float32)
        dense = jnp.einsum('kpq,ckq->ckp', inverse, zmodes, precision=highest)
        back = jnp.einsum('zk,ckp->czp', basis_z, dense, precision=highest) * in_use
        folded = fold_blocks(back, 0, half_patch).reshape(NZ + half_patch, PATCH, PATCH)
        current = lax.dynamic_slice(accum, (anchor, start_x, start_y), (NZ + half_patch, PATCH, PATCH))
        return lax.dynamic_update_slice(accum, current + folded, (anchor, start_x, start_y))

    accum = lax.fori_loop(0, slots, add_cut, accum)
    total = accum[quarter:quarter + NZ, quarter:quarter + NX, quarter:quarter + NY]
    return state + damping * live_mask[None] * total
```

```python
import functools

import jax
import jax.numpy as jnp
from jax import lax
from jax.experimental import pallas as pl
from jax.experimental.pallas import tpu as pltpu
from jax.sharding import PartitionSpec as P

BAND = 4
PATCH = 16
damping = 0.5
FAR = 100000

f32 = jnp.float32
bf16 = jnp.bfloat16
VMEM = pl.BlockSpec(memory_space=pltpu.VMEM)
SMEM = pl.BlockSpec(memory_space=pltpu.SMEM)
HBM = pl.BlockSpec(memory_space=pltpu.HBM)


def split(x):
    hi = x.astype(bf16)
    return hi, (x - hi.astype(f32)).astype(bf16)


def split3(x):
    hi, rest = x.astype(bf16), x
    rest = rest - hi.astype(f32)
    mid = rest.astype(bf16)
    return hi, mid, (rest - mid.astype(f32)).astype(bf16)


def dot(a, b):
    return lax.dot_general(a, b, (((1,), (0,)), ((), ())), preferred_element_type=f32)


def dot_t(a, b):
    return lax.dot_general(a, b, (((1,), (1,)), ((), ())), preferred_element_type=f32)


def dot3(ah, al, bh, bl):
    return dot(ah, bh) + (dot(ah, bl) + dot(al, bh))


def pick(x, onehot):
    h, m, l = split3(x)
    return dot(h, onehot) + dot(m, onehot) + dot(l, onehot)


def place(onehot, x):
    h, m, l = split3(x)
    return dot(onehot, h) + dot(onehot, m) + dot(onehot, l)


def iota(shape, dim):
    return lax.broadcasted_iota(jnp.int32, shape, dim)


def parity(axis):
    return lax.rem(lax.axis_index(axis), 2)


def y_coord(lane, par):
    far = lane * 64 + FAR
    above, below = lane, lane - 136
    first = jnp.where(par == 0, above, below)
    second = jnp.where(par == 0, below - 8, above - 8)
    return jnp.where(
        lane < 128, lane, jnp.where(lane < 136, first, jnp.where(lane < 144, second, far))
    )


def toeplitz(dist, coeffs):
    out = jnp.zeros(dist.shape, f32)
    for k in range(BAND + 1):
        out = jnp.where(dist == k, coeffs[k], out)
    return out


def pack_x_kernel(st, ld, ac, s_out, l_out, send_a, send_b, wide):
    px = parity("gx")
    wide[...] = ld[...].astype(f32)
    for x in range(32):
        s_out[8 * x : 8 * x + 8, :] = st[pl.ds(x, 8, stride=32), :]
        l_out[8 * x : 8 * x + 8, :] = wide[pl.ds(x, 8, stride=32), :]
    act = ac[...].astype(f32)
    low = jnp.concatenate([s_out[0:64, :], l_out[0:32, :], act[0:8]], axis=0)
    high = jnp.concatenate([s_out[192:256, :], l_out[224:256, :], act[24:32]], axis=0)
    send_a[...] = jnp.where(px == 0, high, low)
    send_b[...] = jnp.where(px == 0, low, high)


def pack_y_kernel(s, ld, ac, ra, rb, sw_out, lw_out, send_a, send_b):
    px, py = parity("gx"), parity("gy")
    a, b = ra[...], rb[...]
    low = jnp.where(px == 0, b, a)
    high = jnp.where(px == 0, a, b)
    sw = jnp.concatenate([low[0:64], s[...], high[0:64]], axis=0)
    lw = jnp.concatenate(
        [
            low[64:96],
            ld[...],
            high[64:96],
            low[96:104],
            ac[...].astype(f32),
            high[96:104],
            jnp.zeros((16, 128), f32),
        ],
        axis=0,
    )
    sw_out[...] = sw
    lw_out[...] = lw
    st, lt = sw.T, lw.T
    low_t = jnp.concatenate([st[0:8], lt[0:8]], axis=0)
    high_t = jnp.concatenate([st[120:128], lt[120:128]], axis=0)
    send_a[...] = jnp.where(py == 0, high_t, low_t)
    send_b[...] = jnp.where(py == 0, low_t, high_t)


def build_kernel(
    stiff, mass, basis, values, cols,
    yh, yl, lh, ll, ayh, ayl, ath, atl, kh, kl, kth, ktl, dinv, sel, sel_t, lzh, lzl, lzth, lztl,
):
    py = parity("gy")
    kz, kx, ky = ([stiff[d, k] for k in range(BAND + 1)] for d in range(3))
    mz, mx, my = ([mass[d, k] for k in range(BAND + 1)] for d in range(3))
    dist = jnp.abs(y_coord(iota((256, 256), 0), py) - y_coord(iota((256, 256), 1), py))
    yh[:, 0:256], yl[:, 0:256] = split(toeplitz(dist, my))
    yh[:, 256:512], yl[:, 256:512] = split(toeplitz(dist, ky))
    row, col = iota((64, 128), 0), iota((64, 128), 1)
    dx = jnp.abs((row >> 3) + 4 - (col >> 3))
    dz = jnp.abs((row & 7) - (col & 7))
    tmz, tmx = toeplitz(dz, mz), toeplitz(dx, mx)
    first = tmz * toeplitz(dx, kx) + toeplitz(dz, kz) * tmx
    lh[:, 0:128], ll[:, 0:128] = split(first)
    lh[:, 128:256], ll[:, 128:256] = split(tmz * tmx)
    one = lambda cond: jnp.where(cond, 1.0, 0.0).astype(bf16)
    tile_j = one(iota((16, 256), 0) == (iota((16, 256), 1) & 15))
    vy = pick(basis[2], tile_j)
    c = y_coord(iota((256, 256), 0), py)
    b = iota((256, 256), 1) >> 4
    t = c + 4 - 8 * b
    lower = jnp.concatenate([vy[4:8], vy[0:4]], axis=0)
    upper = jnp.concatenate([vy[12:16], vy[8:12]], axis=0)
    lower = jnp.concatenate([lower] * 32, axis=0)
    upper = jnp.concatenate([upper] * 32, axis=0)
    ay = jnp.where((t >= 0) & (t < 8), lower, jnp.where((t >= 8) & (t < 16), upper, 0.0))
    ayh[...], ayl[...] = split(ay)
    ath[...], atl[...] = split(ay.T)
    to_i = one((iota((256, 16), 0) >> 4) == iota((256, 16), 1))
    to_k = one((iota((256, 16), 0) & 15) == iota((256, 16), 1))
    to_xx = one((iota((16, 128), 1) >> 3) == iota((16, 128), 0))
    to_z = one((iota((16, 128), 1) & 7) + 4 == iota((16, 128), 0))
    vz_rows = pick(basis[0].T, to_z)
    vx_rows = pick(basis[1].T, to_xx)
    kron = place(to_i, vx_rows) * place(to_k, vz_rows)
    kh[...], kl[...] = split(kron)
    kth[...], ktl[...] = split(kron.T)
    lzh[...], lzl[...] = split(vz_rows)
    lzth[...], lztl[...] = split(vz_rows.T)
    lam = values[...]
    lanes = pick(jnp.concatenate([lam, jnp.zeros((5, 16), f32)], axis=0), tile_j)[2:3]
    lam_t = jnp.concatenate([lam, jnp.zeros((5, 16), f32)], axis=0).T
    lam_i, lam_k = place(to_i, lam_t)[:, 1:2], place(to_k, lam_t)[:, 0:1]
    dinv[...] = 1.0 / (lam_k + lam_i + lanes)
    yy = iota((256, 256), 1) & 15
    cy = y_coord(iota((256, 256), 0), py)
    yy_t = iota((256, 256), 0) & 15
    cy_t = y_coord(iota((256, 256), 1), py)
    for m in range(2):
        entry = cols[m]
        at = jnp.where(entry >= 0, 8 * (jnp.maximum(entry, 0) & 15) - 4, -4 * FAR)
        sel[m] = one(cy == yy + at)
        sel_t[m] = one(cy_t == yy_t + at)


def main_kernel(
    cols, sw, lw, ra, rb,
    yh, yl, lh, ll, ayh, ayl, ath, atl, kh, kl, kth, ktl, dinv, sel, sel_t, lzh, lzl, lzth, lztl,
    inverse,
    total_out, send_a, send_b,
    rh, rl, tacc, inv, sem,
):
    fetch = [pltpu.make_async_copy(inverse.at[m], inv.at[m], sem.at[m]) for m in range(2)]
    for copy in fetch:
        copy.start()
    pad = jnp.zeros((112, 384), f32)
    strip = jnp.concatenate([ra[0:8], rb[0:8], pad], axis=0).T
    lstrip = jnp.concatenate([ra[8:16], rb[8:16], pad], axis=0).T
    lwin = lw[...]
    sh, sl = split(jnp.concatenate([sw[...], strip], axis=1))
    syh, syl = split(dot3(sh, sl, yh[...], yl[...]))
    act = jnp.concatenate([lwin[320:384], lstrip[320:384]], axis=1).astype(bf16)
    spread = jnp.where((iota((320, 64), 0) >> 3) + 4 == iota((320, 64), 1), 1.0, 0.0).astype(bf16)
    live = dot(spread, act)
    load = jnp.concatenate([lwin[0:320], lstrip[0:320]], axis=1)
    left_h, left_l = lh[...], ll[...]
    for o in range(5):
        rows = slice(64 * o, 64 * o + 128)
        bh = jnp.concatenate([syh[rows, 0:256], syh[rows, 256:512]], axis=0)
        bl = jnp.concatenate([syl[rows, 0:256], syl[rows, 256:512]], axis=0)
        mine = slice(64 * o, 64 * o + 64)
        rest = live[mine] * (load[mine] - dot3(left_h, left_l, bh, bl))
        rh[mine, :], rl[mine, :] = split(rest)
    ryh, ryl = split(dot3(rh[...], rl[...], ayh[...], ayl[...]))
    tacc[...] = jnp.zeros((320, 256), f32)
    lane_b = iota((1, 256), 1) >> 4
    for a in range(4):
        rows = slice(64 * a, 64 * a + 128)
        modes = dot3(kh[...], kl[...], ryh[rows], ryl[rows])
        keep = jnp.ones((1, 256), f32)
        for m in range(2):
            entry = cols[m]
            keep = jnp.where(lane_b + 16 * a == entry, 0.0, keep)
        mh, ml = split(modes * dinv[...] * keep)
        tacc[rows, :] += dot3(kth[...], ktl[...], mh, ml)
    th, tl = split(tacc[...])
    tacc[...] = dot3(th, tl, ath[...], atl[...])
    same = (iota((128, 256), 0) >> 3) == (iota((128, 256), 1) >> 4)
    for m in range(2):
        at = pl.multiple_of(64 * (jnp.maximum(cols[m], 0) >> 4), 64)
        rows = pl.ds(at, 128)
        cells = dot(rh[rows, :], sel[m]) + dot(rl[rows, :], sel[m])
        ch, cl = split(jnp.where(same, cells, 0.0))
        zmodes = dot3(lzh[...], lzl[...], ch, cl).astype(bf16)
        fetch[m].wait()
        lane_k = iota((256, 16), 1)
        dense = jnp.zeros((256, 16), f32)
        for k in range(16):
            dense = jnp.where(lane_k == k, dot_t(inv[m, k], zmodes), dense)
        dh, dl = split(dense)
        back = dot_t(lzth[...], dh) + (dot_t(lzth[...], dl) + dot_t(lztl[...], dh))
        gh, gl = split(jnp.where(same, back, 0.0))
        tacc[rows, :] += dot(gh, sel_t[m]) + dot(gl, sel_t[m])
    total_out[...] = tacc[:, 0:128]
    edge = jnp.concatenate([tacc[:, 128:256], jnp.zeros((64, 128), f32)], axis=0).T
    send_a[...] = edge[0:8]
    send_b[...] = edge[8:16]


def join_y_kernel(total, ra, rb, core_out, send_a, send_b):
    px, py = parity("gx"), parity("gy")
    low = jnp.where(py == 0, rb[...], ra[...])
    high = jnp.where(py == 0, ra[...], rb[...])
    edge = jnp.concatenate([low, jnp.zeros((112, 384), f32), high], axis=0).T
    full = total[...] + edge[0:320]
    core_out[...] = full[32:288]
    send_a[...] = jnp.where(px == 0, full[288:320], full[0:32])
    send_b[...] = jnp.where(px == 0, full[0:32], full[288:320])


def finish_kernel(core, ra, rb, st, ac, out):
    px = parity("gx")
    low = jnp.where(px == 0, rb[...], ra[...])
    high = jnp.where(px == 0, ra[...], rb[...])
    for x in range(32):
        term = core[8 * x : 8 * x + 8, :]
        if x < 4:
            term = term + low[8 * x : 8 * x + 8]
        if x >= 28:
            term = term + high[8 * (x - 28) : 8 * (x - 28) + 8]
        row = damping * ac[pl.ds(x, 1), :].astype(f32)
        rows = pl.ds(x, 8, stride=32)
        out[rows, :] = st[rows, :] + row * term


def call(kernel, outs, ins, scratch=(), name=None, flops=10**6, limit=8 * 2**20):
    return pl.pallas_call(
        kernel,
        out_shape=[jax.ShapeDtypeStruct(s, t) for s, t in outs],
        in_specs=ins,
        out_specs=[VMEM] * len(outs),
        scratch_shapes=scratch,
        name=name,
        compiler_params=pltpu.CompilerParams(vmem_limit_bytes=limit),
        cost_estimate=pl.CostEstimate(flops=flops, bytes_accessed=10**6, transcendentals=0),
    )


def swaps(axis, first):
    size = lax.axis_size(axis)
    lows = range(first, size - 1, 2)
    return [(i, i + 1) for i in lows] + [(i + 1, i) for i in lows]


def exchange(a, b, axis):
    return lax.ppermute(a, axis, swaps(axis, 0)), lax.ppermute(b, axis, swaps(axis, 1))


def on_device(
    state, load_vector, active, stiff_band, mass_band, eig_basis, eig_values, cut_cols, cut_inverse
):
    st = state.reshape(256, 128)
    ld = load_vector.reshape(256, 128)
    cols = cut_cols.reshape(2)
    inverse = cut_inverse.reshape(2, PATCH, 256, 256)
    s, l, xa, xb = call(
        pack_x_kernel,
        [((256, 128), f32), ((256, 128), f32), ((104, 128), f32), ((104, 128), f32)],
        [VMEM] * 3,
        [pltpu.VMEM((256, 128), f32)],
        name="pack_x",
    )(st, ld, active)
    xa, xb = exchange(xa, xb, "gx")
    sq = ((256, 256), bf16)
    mats = call(
        build_kernel,
        [
            ((256, 512), bf16), ((256, 512), bf16), ((64, 256), bf16), ((64, 256), bf16),
            sq, sq, sq, sq,
            ((256, 128), bf16), ((256, 128), bf16), ((128, 256), bf16), ((128, 256), bf16),
            ((256, 256), f32), ((2, 256, 256), bf16), ((2, 256, 256), bf16),
            ((16, 128), bf16), ((16, 128), bf16), ((128, 16), bf16), ((128, 16), bf16),
        ],
        [SMEM, SMEM, VMEM, VMEM, SMEM],
        name="build",
    )(stiff_band, mass_band, eig_basis, eig_values, cols)
    sw, lw, ya, yb = call(
        pack_y_kernel,
        [((384, 128), f32), ((384, 128), f32), ((16, 384), f32), ((16, 384), f32)],
        [VMEM] * 5,
        name="pack_y",
    )(s, l, active, xa, xb)
    ya, yb = exchange(ya, yb, "gy")
    total, ya, yb = call(
        main_kernel,
        [((320, 128), f32), ((8, 384), f32), ((8, 384), f32)],
        [SMEM] + [VMEM] * 23 + [HBM],
        [
            pltpu.VMEM((320, 256), bf16),
            pltpu.VMEM((320, 256), bf16),
            pltpu.VMEM((320, 256), f32),
            pltpu.VMEM((2, PATCH, 256, 256), bf16),
            pltpu.SemaphoreType.DMA((2,)),
        ],
        name="main",
        limit=20 * 2**20,
    )(cols, sw, lw, ya, yb, *mats, inverse)
    ya, yb = exchange(ya, yb, "gy")
    core, xa, xb = call(
        join_y_kernel,
        [((256, 128), f32), ((32, 128), f32), ((32, 128), f32)],
        [VMEM] * 3,
        name="join_y",
    )(total, ya, yb)
    xa, xb = exchange(xa, xb, "gx")
    (out,) = call(finish_kernel, [((256, 128), f32)], [VMEM] * 5, name="finish")(
        core, xa, xb, st, active
    )
    return out.reshape(8, 32, 128)


def solution(mesh):
    placed = (
        P(None, "gx", "gy"),
        P(None, "gx", "gy"),
        P("gx", "gy"),
        P(),
        P(),
        P(),
        P(),
        P("gx", "gy", None),
        P("gx", "gy", None, None, None, None),
    )
    return jax.shard_map(
        on_device, mesh=mesh, in_specs=placed, out_specs=P(None, "gx", "gy"), check_vma=False
    )
```

```python
import functools

import jax
import jax.numpy as jnp
from jax import lax
from jax.experimental import pallas as pl
from jax.experimental.pallas import tpu as pltpu
from jax.sharding import PartitionSpec as P

BAND = 4
PATCH = 16
damping = 0.5
FAR = 100000

f32 = jnp.float32
bf16 = jnp.bfloat16
VMEM = pl.BlockSpec(memory_space=pltpu.VMEM)
ANY = pl.BlockSpec(memory_space=pl.ANY)


def split(x):
    hi = x.astype(bf16)
    return hi, (x - hi.astype(f32)).astype(bf16)


def split3(x):
    hi, rest = x.astype(bf16), x
    rest = rest - hi.astype(f32)
    mid = rest.astype(bf16)
    return hi, mid, (rest - mid.astype(f32)).astype(bf16)


def dot(a, b):
    return lax.dot_general(a, b, (((1,), (0,)), ((), ())), preferred_element_type=f32)


def dot_t(a, b):
    return lax.dot_general(a, b, (((1,), (1,)), ((), ())), preferred_element_type=f32)


def dot3(ah, al, bh, bl):
    return dot(ah, bh) + (dot(ah, bl) + dot(al, bh))


def pick(x, onehot):
    h, m, l = split3(x)
    return dot(h, onehot) + dot(m, onehot) + dot(l, onehot)


def place(onehot, x):
    h, m, l = split3(x)
    return dot(onehot, h) + dot(onehot, m) + dot(onehot, l)


def iota(shape, dim):
    return lax.broadcasted_iota(jnp.int32, shape, dim)


def parity(axis):
    return lax.rem(lax.axis_index(axis), 2)


def y_coord(lane, par):
    far = lane * 64 + FAR
    above, below = lane, lane - 136
    first = jnp.where(par == 0, above, below)
    second = jnp.where(par == 0, below - 8, above - 8)
    return jnp.where(
        lane < 128, lane, jnp.where(lane < 136, first, jnp.where(lane < 144, second, far))
    )


def toeplitz(dist, coeffs):
    out = jnp.zeros(dist.shape, f32)
    for k in range(BAND + 1):
        out = jnp.where(dist == k, coeffs[k], out)
    return out


def fetch(pairs, sem):
    copies = [pltpu.make_async_copy(a, b, sem.at[n]) for n, (a, b) in enumerate(pairs)]
    for copy in copies:
        copy.start()
    for copy in copies:
        copy.wait()


def either(flag, a, b):
    return jnp.where(flag == 0, a, b)


def pack_y_kernel(
    st_hbm, ld_hbm, ac_hbm, s_out, l_out, a_out, send_a, send_b, st, ld, ac, wide, sem
):
    fetch([(st_hbm, st), (ld_hbm, ld), (ac_hbm, ac)], sem)
    py = parity("gy")
    wide[...] = ld[...].astype(f32)
    for x in range(32):
        s_out[8 * x : 8 * x + 8, :] = st[pl.ds(x, 8, stride=32), :]
        l_out[8 * x : 8 * x + 8, :] = wide[pl.ds(x, 8, stride=32), :]
    act = ac[...].astype(f32)
    a_out[...] = act
    turned = [s_out[...].T, l_out[...].T, jnp.concatenate([act, jnp.zeros((96, 128), f32)], axis=0).T]
    low = jnp.concatenate([t[0:8] for t in turned], axis=1)
    high = jnp.concatenate([t[120:128] for t in turned], axis=1)
    send_a[...] = either(py, high, low)
    send_b[...] = either(py, low, high)


def pack_x_kernel(after, s, l, ac, ra, rb, sw, lw, aw, send_a, send_b):
    del after
    px = parity("gx")

    def strips(lanes, width):
        both = [ra[:, lanes], rb[:, lanes], jnp.zeros((112, width), f32)]
        return jnp.concatenate(both, axis=0).T

    sw[:, 0:128] = s[...]
    sw[:, 128:256] = strips(slice(0, 256), 256)
    lw[:, 0:128] = l[...]
    lw[:, 128:256] = strips(slice(256, 512), 256)
    aw[:, 0:128] = ac[...]
    aw[:, 128:256] = strips(slice(512, 640), 128)[0:32]

    def edge(srow, lrow, arow):
        rows = [sw[srow : srow + 64, :], lw[lrow : lrow + 32, :], aw[arow : arow + 8, :]]
        rows = jnp.concatenate(rows, axis=0)
        corner = jnp.concatenate([rows[:, 128:256], jnp.zeros((24, 128), f32)], axis=0).T
        return jnp.concatenate([rows[:, 0:128], corner[0:16]], axis=0)

    low, high = edge(0, 0, 0), edge(192, 224, 24)
    send_a[...] = either(px, high, low)
    send_b[...] = either(px, low, high)


def stencil(left_h, left_l, syh, syl, live, load):
    bh = jnp.concatenate([syh[:, 0:256], syh[:, 256:512]], axis=0)
    bl = jnp.concatenate([syl[:, 0:256], syl[:, 256:512]], axis=0)
    return split(live * (load - dot3(left_h, left_l, bh, bl)))


def solve_row(a, khl, kth, ktl, dinv, cols, ryh, ryl):
    modes = dot(khl, jnp.concatenate([ryh, ryh], axis=0)) + dot(khl[:, 0:128], ryl)
    lane_b = iota((1, 256), 1) >> 4
    keep = jnp.ones((1, 256), f32)
    for m in range(2):
        keep = jnp.where(lane_b + 16 * a == cols[m], 0.0, keep)
    mh, ml = split(modes * dinv * keep)
    return dot3(kth, ktl, mh, ml)


def inner_kernel(
    cols_hbm, sw, lw, aw, yh, yl, lh, ll, ayh, ayl, khl, kth, ktl, dinv, inverse,
    syh, syl, rh, rl, ryh, ryl, tin, inv, cols, sem,
):
    listed = pltpu.make_async_copy(cols_hbm, cols, sem.at[2])
    listed.start()
    copies = [pltpu.make_async_copy(inverse.at[m], inv.at[m], sem.at[m]) for m in range(2)]
    for copy in copies:
        copy.start()
    sh, sl = split(sw[...])
    syh[...], syl[...] = split(dot3(sh, sl, yh[...], yl[...]))
    spread = jnp.where((iota((192, 32), 0) >> 3) + 4 == iota((192, 32), 1), 1.0, 0.0)
    live = dot(spread.astype(bf16), aw[...].astype(bf16))
    for o in range(3):
        rows, mine = slice(64 * o, 64 * o + 128), slice(64 * o, 64 * o + 64)
        load = lw[64 * o + 32 : 64 * o + 96, :]
        rh[mine, :], rl[mine, :] = stencil(
            lh[...], ll[...], syh[rows, :], syl[rows, :], live[mine], load
        )
    ryh[...], ryl[...] = split(dot3(rh[...], rl[...], ayh[...], ayl[...]))
    listed.wait()
    rest = (khl[...], kth[...], ktl[...], dinv[...], cols)
    one = solve_row(1, *rest, ryh[0:128, :], ryl[0:128, :])
    two = solve_row(2, *rest, ryh[64:192, :], ryl[64:192, :])
    tin[0:64, :] = one[0:64]
    tin[64:128, :] = one[64:128] + two[0:64]
    tin[128:192, :] = two[64:128]
    for copy in copies:
        copy.wait()


def edge_kernel(
    cols_hbm, lw, aw, ra, rb, syh, syl, rh_in, rl_in, ryh, ryl, inv,
    yh, yl, lh, ll, ayh, ayl, ath, atl, khl, kth, ktl, dinv, sel, sel_t, lzh, lzl, lzth, lztl,
    first, last, cut, send_a, send_b, rh, rl, cols, sem,
):
    listed = pltpu.make_async_copy(cols_hbm, cols, sem)
    listed.start()
    px = parity("gx")
    low, high = either(px, rb[...], ra[...]), either(px, ra[...], rb[...])

    def halo(block):
        corner = jnp.concatenate([block[104:120], jnp.zeros((112, 128), f32)], axis=0).T
        return jnp.concatenate([block[0:104], corner[0:104]], axis=1)

    low, high = halo(low), halo(high)
    sh, sl = split(jnp.concatenate([low[0:64], high[0:64]], axis=0))
    ehh, ehl = split(dot3(sh, sl, yh[...], yl[...]))
    spread = jnp.where((iota((64, 16), 0) >> 3) + 4 == iota((64, 16), 1), 1.0, 0.0).astype(bf16)
    rh[64:256, :], rl[64:256, :] = rh_in[...], rl_in[...]
    live = dot(spread, jnp.concatenate([low[96:104], aw[0:8, :]], axis=0).astype(bf16))
    rh[0:64, :], rl[0:64, :] = stencil(
        lh[...],
        ll[...],
        jnp.concatenate([ehh[0:64], syh[0:64, :]], axis=0),
        jnp.concatenate([ehl[0:64], syl[0:64, :]], axis=0),
        live,
        jnp.concatenate([low[64:96], lw[0:32, :]], axis=0),
    )
    live = dot(spread, jnp.concatenate([aw[24:32, :], high[96:104]], axis=0).astype(bf16))
    rh[256:320, :], rl[256:320, :] = stencil(
        lh[...],
        ll[...],
        jnp.concatenate([syh[192:256, :], ehh[64:128]], axis=0),
        jnp.concatenate([syl[192:256, :], ehl[64:128]], axis=0),
        live,
        jnp.concatenate([lw[224:256, :], high[64:96]], axis=0),
    )
    same = (iota((128, 256), 0) >> 3) == (iota((128, 256), 1) >> 4)
    row_k = iota((16, 256), 0)
    listed.wait()
    cut[...] = jnp.zeros((320, 256), f32)
    for m in range(2):
        at = pl.multiple_of(64 * (jnp.maximum(cols[m], 0) >> 4), 64)
        rows = pl.ds(at, 128)
        cells = dot(rh[rows, :], sel[m]) + dot(rl[rows, :], sel[m])
        ch, cl = split(jnp.where(same, cells, 0.0))
        zmodes = dot3(lzh[...], lzl[...], ch, cl)
        dense = jnp.zeros((16, 256), f32)
        for k in range(16):
            single = jnp.where(row_k == k, zmodes, 0.0).astype(bf16)
            dense = dense + dot_t(single, inv[m, k])
        dh, dl = split(dense)
        back = dot3(lzth[...], lztl[...], dh, dl)
        gh, gl = split(jnp.where(same, back, 0.0))
        cut[rows, :] += dot(gh, sel_t[m]) + dot(gl, sel_t[m])
    edges_h = jnp.concatenate([rh[0:64, :], rh[256:320, :]], axis=0)
    edges_l = jnp.concatenate([rl[0:64, :], rl[256:320, :]], axis=0)
    eyh, eyl = split(dot3(edges_h, edges_l, ayh[...], ayl[...]))
    rest = (khl[...], kth[...], ktl[...], dinv[...], cols)
    t0 = solve_row(
        0,
        *rest,
        jnp.concatenate([eyh[0:64], ryh[0:64, :]], axis=0),
        jnp.concatenate([eyl[0:64], ryl[0:64, :]], axis=0),
    )
    t3 = solve_row(
        3,
        *rest,
        jnp.concatenate([ryh[128:192, :], eyh[64:128]], axis=0),
        jnp.concatenate([ryl[128:192, :], eyl[64:128]], axis=0),
    )
    first[...], last[...] = t0[32:128], t3[0:96]
    th, tl = split(jnp.concatenate([t0[0:32], t3[96:128]], axis=0))
    out = dot3(th, tl, ath[...], atl[...])
    out_low, out_high = out[0:32] + cut[0:32, :], out[32:64] + cut[288:320, :]
    pad = jnp.zeros((96, 128), f32)
    corner_low = jnp.concatenate([pad, out_low[:, 128:256]], axis=0).T
    corner_high = jnp.concatenate([out_high[:, 128:256], pad], axis=0).T
    out_low = jnp.concatenate([out_low[:, 0:128], corner_low[0:16]], axis=0)
    out_high = jnp.concatenate([out_high[:, 0:128], corner_high[0:16]], axis=0)
    send_a[...] = either(px, out_high, out_low)
    send_b[...] = either(px, out_low, out_high)


def spread_kernel(first, last, tin, cut, ath, atl, core, side):
    total = jnp.concatenate(
        [
            first[0:32, :],
            first[32:96, :] + tin[0:64, :],
            tin[64:128, :],
            tin[128:192, :] + last[0:64, :],
            last[64:96, :],
        ],
        axis=0,
    )
    th, tl = split(total)
    total = dot3(th, tl, ath[...], atl[...]) + cut[32:288, :]
    core[...] = total[:, 0:128]
    side[...] = total[:, 128:256].T[0:16]


def join_x_kernel(side, ra, rb, send_a, send_b):
    px = parity("gx")
    low, high = either(px, rb[32:48, :], ra[32:48, :]), either(px, ra[32:48, :], rb[32:48, :])
    full = side[...] + jnp.concatenate([low, high], axis=1)
    send_a[...] = full[0:8]
    send_b[...] = full[8:16]


def finish_kernel(core, xa, xb, ya, yb, s, ac, out):
    px, py = parity("gx"), parity("gy")
    low, high = either(px, xb[0:32, :], xa[0:32, :]), either(px, xa[0:32, :], xb[0:32, :])
    left, right = either(py, yb[...], ya[...]), either(py, ya[...], yb[...])
    edge = jnp.concatenate([left, jnp.zeros((112, 256), f32), right], axis=0).T
    total = core[...] + edge
    for x in range(32):
        term = total[8 * x : 8 * x + 8]
        if x < 4:
            term = term + low[8 * x : 8 * x + 8]
        if x >= 28:
            term = term + high[8 * (x - 28) : 8 * (x - 28) + 8]
        row = damping * ac[pl.ds(x, 1), :]
        out[pl.ds(x, 8, stride=32), :] = s[8 * x : 8 * x + 8, :] + row * term


def build_kernel(
    after, stiff_hbm, mass_hbm, basis_hbm, values_hbm, cols_hbm,
    yh, yl, lh, ll, ayh, ayl, ath, atl, khl, kth, ktl, dinv, sel, sel_t, lzh, lzl, lzth, lztl,
    stiff, mass, basis, values, cols, sem,
):
    del after
    fetch(
        [
            (stiff_hbm, stiff),
            (mass_hbm, mass),
            (basis_hbm, basis),
            (values_hbm, values),
            (cols_hbm, cols),
        ],
        sem,
    )
    py = parity("gy")
    kz, kx, ky = ([stiff[d, k] for k in range(BAND + 1)] for d in range(3))
    mz, mx, my = ([mass[d, k] for k in range(BAND + 1)] for d in range(3))
    dist = jnp.abs(y_coord(iota((256, 256), 0), py) - y_coord(iota((256, 256), 1), py))
    yh[:, 0:256], yl[:, 0:256] = split(toeplitz(dist, my))
    yh[:, 256:512], yl[:, 256:512] = split(toeplitz(dist, ky))
    row, col = iota((64, 128), 0), iota((64, 128), 1)
    dx = jnp.abs((row >> 3) + 4 - (col >> 3))
    dz = jnp.abs((row & 7) - (col & 7))
    tmz, tmx = toeplitz(dz, mz), toeplitz(dx, mx)
    first = tmz * toeplitz(dx, kx) + toeplitz(dz, kz) * tmx
    lh[:, 0:128], ll[:, 0:128] = split(first)
    lh[:, 128:256], ll[:, 128:256] = split(tmz * tmx)
    one = lambda cond: jnp.where(cond, 1.0, 0.0).astype(bf16)
    tile_j = one(iota((16, 256), 0) == (iota((16, 256), 1) & 15))
    vy = pick(basis[2], tile_j)
    c = y_coord(iota((256, 256), 0), py)
    b = iota((256, 256), 1) >> 4
    t = c + 4 - 8 * b
    lower = jnp.concatenate([vy[4:8], vy[0:4]], axis=0)
    upper = jnp.concatenate([vy[12:16], vy[8:12]], axis=0)
    lower = jnp.concatenate([lower] * 32, axis=0)
    upper = jnp.concatenate([upper] * 32, axis=0)
    ay = jnp.where((t >= 0) & (t < 8), lower, jnp.where((t >= 8) & (t < 16), upper, 0.0))
    ayh[...], ayl[...] = split(ay)
    ath[...], atl[...] = split(ay.T)
    to_i = one((iota((256, 16), 0) >> 4) == iota((256, 16), 1))
    to_k = one((iota((256, 16), 0) & 15) == iota((256, 16), 1))
    to_xx = one((iota((16, 128), 1) >> 3) == iota((16, 128), 0))
    to_z = one((iota((16, 128), 1) & 7) + 4 == iota((16, 128), 0))
    vz_rows = pick(basis[0].T, to_z)
    vx_rows = pick(basis[1].T, to_xx)
    kron = place(to_i, vx_rows) * place(to_k, vz_rows)
    khl[:, 0:128], khl[:, 128:256] = split(kron)
    kth[...], ktl[...] = split(kron.T)
    lzh[...], lzl[...] = split(vz_rows)
    lzth[...], lztl[...] = split(vz_rows.T)
    lam = values[...]
    lanes = pick(jnp.concatenate([lam, jnp.zeros((5, 16), f32)], axis=0), tile_j)[2:3]
    lam_t = jnp.concatenate([lam, jnp.zeros((5, 16), f32)], axis=0).T
    lam_i, lam_k = place(to_i, lam_t)[:, 1:2], place(to_k, lam_t)[:, 0:1]
    dinv[...] = 1.0 / (lam_k + lam_i + lanes)
    yy = iota((256, 256), 1) & 15
    cy = y_coord(iota((256, 256), 0), py)
    yy_t = iota((256, 256), 0) & 15
    cy_t = y_coord(iota((256, 256), 1), py)
    for m in range(2):
        entry = cols[m]
        at = jnp.where(entry >= 0, 8 * (jnp.maximum(entry, 0) & 15) - 4, -4 * FAR)
        sel[m] = one(cy == yy + at)
        sel_t[m] = one(cy_t == yy_t + at)


def call(kernel, outs, ins, scratch=(), name=None, flops=10**6, limit=8 * 2**20):
    return pl.pallas_call(
        kernel,
        out_shape=[jax.ShapeDtypeStruct(s, t) for s, t in outs],
        in_specs=ins,
        out_specs=[VMEM] * len(outs),
        scratch_shapes=scratch,
        name=name,
        compiler_params=pltpu.CompilerParams(vmem_limit_bytes=limit),
        cost_estimate=pl.CostEstimate(flops=flops, bytes_accessed=10**6, transcendentals=0),
    )


def swaps(axis, first):
    size = lax.axis_size(axis)
    lows = range(first, size - 1, 2)
    return [(i, i + 1) for i in lows] + [(i + 1, i) for i in lows]


def exchange(a, b, axis):
    return lax.ppermute(a, axis, swaps(axis, 0)), lax.ppermute(b, axis, swaps(axis, 1))


def on_device(
    state, load_vector, active, stiff_band, mass_band, eig_basis, eig_values, cut_cols, cut_inverse
):
    st, ld, active, stiff, mass, basis, values, cols_in, inverse = (
        pltpu.with_memory_space_constraint(x, pltpu.HBM)
        for x in (
            state.reshape(256, 128),
            load_vector.reshape(256, 128),
            active,
            stiff_band,
            mass_band,
            eig_basis,
            eig_values,
            cut_cols.reshape(2),
            cut_inverse.reshape(2, PATCH, 256, 256),
        )
    )
    dma = pltpu.SemaphoreType.DMA
    s, l, ac, ya, yb = call(
        pack_y_kernel,
        [((256, 128), f32), ((256, 128), f32), ((32, 128), f32), ((8, 640), f32), ((8, 640), f32)],
        [ANY] * 3,
        [
            pltpu.VMEM((256, 128), f32),
            pltpu.VMEM((256, 128), bf16),
            pltpu.VMEM((32, 128), jnp.int32),
            pltpu.VMEM((256, 128), f32),
            dma((3,)),
        ],
        name="pack_y",
        limit=8 * 2**20,
    )(st, ld, active)
    ya, yb = exchange(ya, yb, "gy")
    sq = ((256, 256), bf16)
    yh, yl, lh, ll, ayh, ayl, ath, atl, khl, kth, ktl, dinv, *cutters = call(
        build_kernel,
        [
            ((256, 512), bf16), ((256, 512), bf16), ((64, 256), bf16), ((64, 256), bf16),
            sq, sq, sq, sq,
            sq, ((128, 256), bf16), ((128, 256), bf16),
            ((256, 256), f32), ((2, 256, 256), bf16), ((2, 256, 256), bf16),
            ((16, 128), bf16), ((16, 128), bf16), ((128, 16), bf16), ((128, 16), bf16),
        ],
        [VMEM] + [ANY] * 5,
        [
            pltpu.SMEM((3, 5), f32),
            pltpu.SMEM((3, 5), f32),
            pltpu.VMEM((3, 16, 16), f32),
            pltpu.VMEM((3, 16), f32),
            pltpu.SMEM((2,), jnp.int32),
            dma((5,)),
        ],
        name="build",
        limit=8 * 2**20,
    )(ac, stiff, mass, basis, values, cols_in)
    sw, lw, aw, xa, xb = call(
        pack_x_kernel,
        [((256, 256), f32), ((256, 256), f32), ((32, 256), f32), ((120, 128), f32), ((120, 128), f32)],
        [VMEM] * 6,
        name="pack_x",
    )(lh, s, l, ac, ya, yb)
    xa, xb = exchange(xa, xb, "gx")
    syh, syl, rh, rl, ryh, ryl, tin, inv = call(
        inner_kernel,
        [
            ((256, 512), bf16), ((256, 512), bf16),
            ((192, 256), bf16), ((192, 256), bf16), ((192, 256), bf16), ((192, 256), bf16),
            ((192, 256), f32), ((2, PATCH, 256, 256), bf16),
        ],
        [ANY] + [VMEM] * 13 + [ANY],
        [pltpu.SMEM((2,), jnp.int32), dma((3,))],
        name="inner",
        limit=12 * 2**20,
    )(cols_in, sw, lw, aw, yh, yl, lh, ll, ayh, ayl, khl, kth, ktl, dinv, inverse)
    first, last, cut, xa, xb = call(
        edge_kernel,
        [
            ((96, 256), f32), ((96, 256), f32), ((320, 256), f32),
            ((48, 128), f32), ((48, 128), f32),
        ],
        [ANY] + [VMEM] * 29,
        [
            pltpu.VMEM((320, 256), bf16),
            pltpu.VMEM((320, 256), bf16),
            pltpu.SMEM((2,), jnp.int32),
            dma,
        ],
        name="edge",
    )(
        cols_in, lw, aw, xa, xb, syh, syl, rh, rl, ryh, ryl, inv,
        yh, yl, lh, ll, ayh, ayl, ath, atl, khl, kth, ktl, dinv, *cutters,
    )
    xa, xb = exchange(xa, xb, "gx")
    core, side = call(
        spread_kernel, [((256, 128), f32), ((16, 256), f32)], [VMEM] * 6, name="spread"
    )(first, last, tin, cut, ath, atl)
    ya, yb = call(
        join_x_kernel, [((8, 256), f32), ((8, 256), f32)], [VMEM] * 3, name="join_x"
    )(side, xa, xb)
    ya, yb = exchange(ya, yb, "gy")
    (out,) = call(finish_kernel, [((256, 128), f32)], [VMEM] * 7, name="finish")(
        core, xa, xb, ya, yb, s, ac
    )
    return out.reshape(8, 32, 128)


def solution(mesh):
    placed = (
        P(None, "gx", "gy"),
        P(None, "gx", "gy"),
        P("gx", "gy"),
        P(),
        P(),
        P(),
        P(),
        P("gx", "gy", None),
        P("gx", "gy", None, None, None, None),
    )
    return jax.shard_map(
        on_device, mesh=mesh, in_specs=placed, out_specs=P(None, "gx", "gy"), check_vma=False
    )
```

```python
import functools

import jax
import jax.numpy as jnp
from jax import lax
from jax.experimental import pallas as pl
from jax.experimental.pallas import tpu as pltpu
from jax.sharding import PartitionSpec as P

BAND = 4
PATCH = 16
damping = 0.5
FAR = 100000

f32 = jnp.float32
bf16 = jnp.bfloat16
VMEM = pl.BlockSpec(memory_space=pltpu.VMEM)
ANY = pl.BlockSpec(memory_space=pl.ANY)


def split(x):
    hi = x.astype(bf16)
    return hi, (x - hi.astype(f32)).astype(bf16)


def split3(x):
    hi, rest = x.astype(bf16), x
    rest = rest - hi.astype(f32)
    mid = rest.astype(bf16)
    return hi, mid, (rest - mid.astype(f32)).astype(bf16)


def dot(a, b):
    return lax.dot_general(a, b, (((1,), (0,)), ((), ())), preferred_element_type=f32)


def dot_t(a, b):
    return lax.dot_general(a, b, (((1,), (1,)), ((), ())), preferred_element_type=f32)


def dot3(ah, al, bh, bl):
    return dot(ah, bh) + (dot(ah, bl) + dot(al, bh))


def pick(x, onehot):
    h, m, l = split3(x)
    return dot(h, onehot) + dot(m, onehot) + dot(l, onehot)


def place(onehot, x):
    h, m, l = split3(x)
    return dot(onehot, h) + dot(onehot, m) + dot(onehot, l)


def iota(shape, dim):
    return lax.broadcasted_iota(jnp.int32, shape, dim)


def parity(axis):
    return lax.rem(lax.axis_index(axis), 2)


def y_coord(lane, par):
    far = lane * 64 + FAR
    above, below = lane, lane - 136
    first = jnp.where(par == 0, above, below)
    second = jnp.where(par == 0, below - 8, above - 8)
    return jnp.where(
        lane < 128, lane, jnp.where(lane < 136, first, jnp.where(lane < 144, second, far))
    )


def toeplitz(dist, coeffs):
    out = jnp.zeros(dist.shape, f32)
    for k in range(BAND + 1):
        out = jnp.where(dist == k, coeffs[k], out)
    return out


def fetch(pairs, sem):
    copies = [pltpu.make_async_copy(a, b, sem.at[n]) for n, (a, b) in enumerate(pairs)]
    for copy in copies:
        copy.start()
    for copy in copies:
        copy.wait()


def either(flag, a, b):
    return jnp.where(flag == 0, a, b)


def pack_y_kernel(
    st_hbm, ld_hbm, ac_hbm, s_out, l_out, a_out, send_a, send_b, st, ld, ac, wide, sem
):
    fetch([(st_hbm, st), (ld_hbm, ld), (ac_hbm, ac)], sem)
    py = parity("gy")
    wide[...] = ld[...].astype(f32)
    for x in range(32):
        s_out[8 * x : 8 * x + 8, :] = st[pl.ds(x, 8, stride=32), :]
        l_out[8 * x : 8 * x + 8, :] = wide[pl.ds(x, 8, stride=32), :]
    act = ac[...].astype(f32)
    a_out[...] = act
    turned = [s_out[...].T, l_out[...].T, jnp.concatenate([act, jnp.zeros((96, 128), f32)], axis=0).T]
    low = jnp.concatenate([t[0:8] for t in turned], axis=1)
    high = jnp.concatenate([t[120:128] for t in turned], axis=1)
    send_a[...] = either(py, high, low)
    send_b[...] = either(py, low, high)


def pack_x_kernel(after, s, l, ac, ra, rb, sw, lw, aw, send_a, send_b):
    del after
    px = parity("gx")

    def strips(lanes, width):
        both = [ra[:, lanes], rb[:, lanes], jnp.zeros((112, width), f32)]
        return jnp.concatenate(both, axis=0).T

    sw[:, 0:128] = s[...]
    sw[:, 128:256] = strips(slice(0, 256), 256)
    lw[:, 0:128] = l[...]
    lw[:, 128:256] = strips(slice(256, 512), 256)
    aw[:, 0:128] = ac[...]
    aw[:, 128:256] = strips(slice(512, 640), 128)[0:32]

    def edge(srow, lrow, arow):
        rows = [sw[srow : srow + 64, :], lw[lrow : lrow + 32, :], aw[arow : arow + 8, :]]
        rows = jnp.concatenate(rows, axis=0)
        corner = jnp.concatenate([rows[:, 128:256], jnp.zeros((24, 128), f32)], axis=0).T
        return jnp.concatenate([rows[:, 0:128], corner[0:16]], axis=0)

    low, high = edge(0, 0, 0), edge(192, 224, 24)
    send_a[...] = either(px, high, low)
    send_b[...] = either(px, low, high)


def stencil(left_h, left_l, syh, syl, live, load):
    bh = jnp.concatenate([syh[:, 0:256], syh[:, 256:512]], axis=0)
    bl = jnp.concatenate([syl[:, 0:256], syl[:, 256:512]], axis=0)
    return split(live * (load - dot3(left_h, left_l, bh, bl)))


def solve_row(a, khl, kth, ktl, dinv, listed, ryh, ryl):
    modes = dot(khl, jnp.concatenate([ryh, ryh], axis=0)) + dot(khl[:, 0:128], ryl)
    lane_b = iota((1, 256), 1) >> 4
    keep = jnp.ones((1, 256), f32)
    for m in range(2):
        entry = jnp.concatenate([listed[8 * m : 8 * m + 1]] * 2, axis=1)
        keep = jnp.where(lane_b + 16 * a == entry, 0.0, keep)
    mh, ml = split(modes * dinv * keep)
    return dot3(kth, ktl, mh, ml)


def column_cells(rows, rh, rl, sel, lzh, lzl, same):
    cells = dot(rh[rows, :], sel) + dot(rl[rows, :], sel)
    ch, cl = split(jnp.where(same, cells, 0.0))
    return dot3(lzh, lzl, ch, cl)


def cut_column(m, here, entry, rh, rl, sel, sel_t, lzh, lzl, lzth, lztl, inv, cut):
    @pl.when((entry >= 0) & here)
    def _():
        same = (iota((128, 256), 0) >> 3) == (iota((128, 256), 1) >> 4)
        row_k = iota((16, 256), 0)
        rows = pl.ds(pl.multiple_of(64 * (entry >> 4), 64), 128)
        zmodes = column_cells(rows, rh, rl, sel[m], lzh[...], lzl[...], same)
        dense = jnp.zeros((16, 256), f32)
        for k in range(16):
            single = jnp.where(row_k == k, zmodes, 0.0).astype(bf16)
            dense = dense + dot_t(single, inv[k])
        dh, dl = split(dense)
        back = dot3(lzth[...], lztl[...], dh, dl)
        gh, gl = split(jnp.where(same, back, 0.0))
        cut[rows, :] += dot(gh, sel_t[m]) + dot(gl, sel_t[m])


def is_late_row():
    return lax.axis_index("gx") == lax.axis_size("gx") // 2


def inner_work(
    sw, lw, aw, yh, yl, lh, ll, ayh, ayl, khl, kth, ktl, dinv, listed, inverse,
    syh, syl, rh, rl, ryh, ryl, tin, inv, sem,
):
    bulk = pltpu.make_async_copy(inverse.at[1], inv, sem)
    bulk.start()
    sh, sl = split(sw[...])
    syh[...], syl[...] = split(dot3(sh, sl, yh[...], yl[...]))
    spread = jnp.where((iota((192, 32), 0) >> 3) + 4 == iota((192, 32), 1), 1.0, 0.0)
    live = dot(spread.astype(bf16), aw[...].astype(bf16))
    rh[0:64, :] = jnp.zeros((64, 256), bf16)
    rl[0:64, :] = jnp.zeros((64, 256), bf16)
    rh[256:320, :] = jnp.zeros((64, 256), bf16)
    rl[256:320, :] = jnp.zeros((64, 256), bf16)
    for o in range(3):
        rows, mine = slice(64 * o, 64 * o + 128), slice(64 * o, 64 * o + 64)
        load = lw[64 * o + 32 : 64 * o + 96, :]
        into = slice(64 * o + 64, 64 * o + 128)
        rh[into, :], rl[into, :] = stencil(
            lh[...], ll[...], syh[rows, :], syl[rows, :], live[mine], load
        )
    ryh[...], ryl[...] = split(dot3(rh[64:256, :], rl[64:256, :], ayh[...], ayl[...]))
    rest = (khl[...], kth[...], ktl[...], dinv[...], listed[...])
    one = solve_row(1, *rest, ryh[0:128, :], ryl[0:128, :])
    two = solve_row(2, *rest, ryh[64:192, :], ryl[64:192, :])
    tin[0:64, :] = one[0:64]
    tin[64:128, :] = one[64:128] + two[0:64]
    tin[128:192, :] = two[64:128]
    bulk.wait()


def inner_early_kernel(*refs):
    held, send, args, outs, sem = refs[15], refs[24], refs[:15], refs[16:24], refs[25]
    send[...] = held[...]

    @pl.when(is_late_row())
    def _():
        inner_work(*args, *outs, sem)


def inner_kernel(*refs):
    args, outs, sem = refs[:15], refs[23:31], refs[31]

    @pl.when(jnp.logical_not(is_late_row()))
    def _():
        inner_work(*args, *outs, sem)


def edge_kernel(
    cols_hbm, lw, aw, ra, rb, syh, syl, rh_in, rl_in, ryh, ryl, inv0, inv1, listed,
    yh, yl, lh, ll, ayh, ayl, ath, atl, khl, kth, ktl, dinv, sel, sel_t, lzh, lzl, lzth, lztl,
    first, last, cut, send_a, send_b, rh, rl, cols, sem,
):
    fetch_cols = pltpu.make_async_copy(cols_hbm, cols, sem)
    fetch_cols.start()
    px = parity("gx")
    low, high = either(px, rb[...], ra[...]), either(px, ra[...], rb[...])

    def halo(block):
        corner = jnp.concatenate([block[104:120], jnp.zeros((112, 128), f32)], axis=0).T
        return jnp.concatenate([block[0:104], corner[0:104]], axis=1)

    low, high = halo(low), halo(high)
    sh, sl = split(jnp.concatenate([low[0:64], high[0:64]], axis=0))
    ehh, ehl = split(dot3(sh, sl, yh[...], yl[...]))
    spread = jnp.where((iota((64, 16), 0) >> 3) + 4 == iota((64, 16), 1), 1.0, 0.0).astype(bf16)
    rh[64:256, :], rl[64:256, :] = rh_in[64:256, :], rl_in[64:256, :]
    live = dot(spread, jnp.concatenate([low[96:104], aw[0:8, :]], axis=0).astype(bf16))
    rh[0:64, :], rl[0:64, :] = stencil(
        lh[...],
        ll[...],
        jnp.concatenate([ehh[0:64], syh[0:64, :]], axis=0),
        jnp.concatenate([ehl[0:64], syl[0:64, :]], axis=0),
        live,
        jnp.concatenate([low[64:96], lw[0:32, :]], axis=0),
    )
    live = dot(spread, jnp.concatenate([aw[24:32, :], high[96:104]], axis=0).astype(bf16))
    rh[256:320, :], rl[256:320, :] = stencil(
        lh[...],
        ll[...],
        jnp.concatenate([syh[192:256, :], ehh[64:128]], axis=0),
        jnp.concatenate([syl[192:256, :], ehl[64:128]], axis=0),
        live,
        jnp.concatenate([lw[224:256, :], high[64:96]], axis=0),
    )
    cut[...] = jnp.zeros((320, 256), f32)
    edges_h = jnp.concatenate([rh[0:64, :], rh[256:320, :]], axis=0)
    edges_l = jnp.concatenate([rl[0:64, :], rl[256:320, :]], axis=0)
    eyh, eyl = split(dot3(edges_h, edges_l, ayh[...], ayl[...]))
    rest = (khl[...], kth[...], ktl[...], dinv[...], listed[...])
    t0 = solve_row(
        0,
        *rest,
        jnp.concatenate([eyh[0:64], ryh[0:64, :]], axis=0),
        jnp.concatenate([eyl[0:64], ryl[0:64, :]], axis=0),
    )
    t3 = solve_row(
        3,
        *rest,
        jnp.concatenate([ryh[128:192, :], eyh[64:128]], axis=0),
        jnp.concatenate([ryl[128:192, :], eyl[64:128]], axis=0),
    )
    first[...], last[...] = t0[32:128], t3[0:96]
    th, tl = split(jnp.concatenate([t0[0:32], t3[96:128]], axis=0))
    out = dot3(th, tl, ath[...], atl[...])
    fetch_cols.wait()
    for m, inv in enumerate((inv0, inv1)):
        a = cols[m] >> 4
        outer = (a == 0) | (a == 3)
        cut_column(m, outer, cols[m], rh, rl, sel, sel_t, lzh, lzl, lzth, lztl, inv, cut)
    out_low, out_high = out[0:32] + cut[0:32, :], out[32:64] + cut[288:320, :]
    pad = jnp.zeros((96, 128), f32)
    corner_low = jnp.concatenate([pad, out_low[:, 128:256]], axis=0).T
    corner_high = jnp.concatenate([out_high[:, 128:256], pad], axis=0).T
    out_low = jnp.concatenate([out_low[:, 0:128], corner_low[0:16]], axis=0)
    out_high = jnp.concatenate([out_high[:, 0:128], corner_high[0:16]], axis=0)
    send_a[...] = either(px, out_high, out_low)
    send_b[...] = either(px, out_low, out_high)


def spread_kernel(
    cols_hbm, first, last, tin, cut_in, ath, atl, rh, rl, inv0, inv1,
    sel, sel_t, lzh, lzl, lzth, lztl, core, side, cut, cols, sem,
):
    fetch_cols = pltpu.make_async_copy(cols_hbm, cols, sem)
    fetch_cols.start()
    cut[...] = cut_in[...]
    total = jnp.concatenate(
        [
            first[0:32, :],
            first[32:96, :] + tin[0:64, :],
            tin[64:128, :],
            tin[128:192, :] + last[0:64, :],
            last[64:96, :],
        ],
        axis=0,
    )
    th, tl = split(total)
    total = dot3(th, tl, ath[...], atl[...])
    fetch_cols.wait()
    for m, inv in enumerate((inv0, inv1)):
        a = cols[m] >> 4
        middle = (a == 1) | (a == 2)
        cut_column(m, middle, cols[m], rh, rl, sel, sel_t, lzh, lzl, lzth, lztl, inv, cut)
    total = total + cut[32:288, :]
    core[...] = total[:, 0:128]
    side[...] = total[:, 128:256].T[0:16]


def join_x_kernel(side, ra, rb, send_a, send_b):
    px = parity("gx")
    low, high = either(px, rb[32:48, :], ra[32:48, :]), either(px, ra[32:48, :], rb[32:48, :])
    full = side[...] + jnp.concatenate([low, high], axis=1)
    send_a[...] = full[0:8]
    send_b[...] = full[8:16]


def finish_kernel(core, xa, xb, ya, yb, s, ac, out):
    px, py = parity("gx"), parity("gy")
    low, high = either(px, xb[0:32, :], xa[0:32, :]), either(px, xa[0:32, :], xb[0:32, :])
    left, right = either(py, yb[...], ya[...]), either(py, ya[...], yb[...])
    edge = jnp.concatenate([left, jnp.zeros((112, 256), f32), right], axis=0).T
    total = core[...] + edge
    for x in range(32):
        term = total[8 * x : 8 * x + 8]
        if x < 4:
            term = term + low[8 * x : 8 * x + 8]
        if x >= 28:
            term = term + high[8 * (x - 28) : 8 * (x - 28) + 8]
        row = damping * ac[pl.ds(x, 1), :]
        out[pl.ds(x, 8, stride=32), :] = s[8 * x : 8 * x + 8, :] + row * term


def build_kernel(
    after, stiff_hbm, mass_hbm, basis_hbm, values_hbm, cols_hbm, inverse,
    yh, yl, lh, ll, ayh, ayl, ath, atl, khl, kth, ktl, dinv, sel, sel_t, lzh, lzl, lzth, lztl, inv, listed,
    stiff, mass, basis, values, cols, sem,
):
    del after
    bulk = pltpu.make_async_copy(inverse.at[0], inv, sem.at[5])
    bulk.start()
    fetch(
        [
            (stiff_hbm, stiff),
            (mass_hbm, mass),
            (basis_hbm, basis),
            (values_hbm, values),
            (cols_hbm, cols),
        ],
        sem,
    )
    py = parity("gy")
    kz, kx, ky = ([stiff[d, k] for k in range(BAND + 1)] for d in range(3))
    mz, mx, my = ([mass[d, k] for k in range(BAND + 1)] for d in range(3))
    dist = jnp.abs(y_coord(iota((256, 256), 0), py) - y_coord(iota((256, 256), 1), py))
    yh[:, 0:256], yl[:, 0:256] = split(toeplitz(dist, my))
    yh[:, 256:512], yl[:, 256:512] = split(toeplitz(dist, ky))
    row, col = iota((64, 128), 0), iota((64, 128), 1)
    dx = jnp.abs((row >> 3) + 4 - (col >> 3))
    dz = jnp.abs((row & 7) - (col & 7))
    tmz, tmx = toeplitz(dz, mz), toeplitz(dx, mx)
    first = tmz * toeplitz(dx, kx) + toeplitz(dz, kz) * tmx
    lh[:, 0:128], ll[:, 0:128] = split(first)
    lh[:, 128:256], ll[:, 128:256] = split(tmz * tmx)
    one = lambda cond: jnp.where(cond, 1.0, 0.0).astype(bf16)
    tile_j = one(iota((16, 256), 0) == (iota((16, 256), 1) & 15))
    vy = pick(basis[2], tile_j)
    c = y_coord(iota((256, 256), 0), py)
    b = iota((256, 256), 1) >> 4
    t = c + 4 - 8 * b
    lower = jnp.concatenate([vy[4:8], vy[0:4]], axis=0)
    upper = jnp.concatenate([vy[12:16], vy[8:12]], axis=0)
    lower = jnp.concatenate([lower] * 32, axis=0)
    upper = jnp.concatenate([upper] * 32, axis=0)
    ay = jnp.where((t >= 0) & (t < 8), lower, jnp.where((t >= 8) & (t < 16), upper, 0.0))
    ayh[...], ayl[...] = split(ay)
    ath[...], atl[...] = split(ay.T)
    to_i = one((iota((256, 16), 0) >> 4) == iota((256, 16), 1))
    to_k = one((iota((256, 16), 0) & 15) == iota((256, 16), 1))
    to_xx = one((iota((16, 128), 1) >> 3) == iota((16, 128), 0))
    to_z = one((iota((16, 128), 1) & 7) + 4 == iota((16, 128), 0))
    vz_rows = pick(basis[0].T, to_z)
    vx_rows = pick(basis[1].T, to_xx)
    kron = place(to_i, vx_rows) * place(to_k, vz_rows)
    khl[:, 0:128], khl[:, 128:256] = split(kron)
    kth[...], ktl[...] = split(kron.T)
    lzh[...], lzl[...] = split(vz_rows)
    lzth[...], lztl[...] = split(vz_rows.T)
    lam = values[...]
    lanes = pick(jnp.concatenate([lam, jnp.zeros((5, 16), f32)], axis=0), tile_j)[2:3]
    lam_t = jnp.concatenate([lam, jnp.zeros((5, 16), f32)], axis=0).T
    lam_i, lam_k = place(to_i, lam_t)[:, 1:2], place(to_k, lam_t)[:, 0:1]
    dinv[...] = 1.0 / (lam_k + lam_i + lanes)
    yy = iota((256, 256), 1) & 15
    cy = y_coord(iota((256, 256), 0), py)
    yy_t = iota((256, 256), 0) & 15
    cy_t = y_coord(iota((256, 256), 1), py)
    for m in range(2):
        entry = cols[m]
        at = jnp.where(entry >= 0, 8 * (jnp.maximum(entry, 0) & 15) - 4, -4 * FAR)
        sel[m] = one(cy == yy + at)
        sel_t[m] = one(cy_t == yy_t + at)
        listed[8 * m : 8 * m + 8, :] = jnp.full((8, 128), entry, jnp.int32)
    bulk.wait()


def call(kernel, outs, ins, scratch=(), name=None, aliases=None, limit=8 * 2**20):
    return pl.pallas_call(
        kernel,
        out_shape=[jax.ShapeDtypeStruct(s, t) for s, t in outs],
        in_specs=ins,
        out_specs=[VMEM] * len(outs),
        scratch_shapes=scratch,
        name=name,
        compiler_params=pltpu.CompilerParams(vmem_limit_bytes=limit),
        input_output_aliases=aliases or {},
        cost_estimate=pl.CostEstimate(flops=10**6, bytes_accessed=10**6, transcendentals=0),
    )


def swaps(axis, first):
    size = lax.axis_size(axis)
    lows = range(first, size - 1, 2)
    return [(i, i + 1) for i in lows] + [(i + 1, i) for i in lows]


def exchange(a, b, axis):
    return lax.ppermute(a, axis, swaps(axis, 0)), lax.ppermute(b, axis, swaps(axis, 1))


def on_device(
    state, load_vector, active, stiff_band, mass_band, eig_basis, eig_values, cut_cols, cut_inverse
):
    st, ld, active, stiff, mass, basis, values, cols_in, inverse = (
        pltpu.with_memory_space_constraint(x, pltpu.HBM)
        for x in (
            state.reshape(256, 128),
            load_vector.reshape(256, 128),
            active,
            stiff_band,
            mass_band,
            eig_basis,
            eig_values,
            cut_cols.reshape(2),
            cut_inverse.reshape(2, PATCH, 256, 256),
        )
    )
    dma = pltpu.SemaphoreType.DMA
    s, l, ac, ya, yb = call(
        pack_y_kernel,
        [((256, 128), f32), ((256, 128), f32), ((32, 128), f32), ((8, 640), f32), ((8, 640), f32)],
        [ANY] * 3,
        [
            pltpu.VMEM((256, 128), f32),
            pltpu.VMEM((256, 128), bf16),
            pltpu.VMEM((32, 128), jnp.int32),
            pltpu.VMEM((256, 128), f32),
            dma((3,)),
        ],
        name="pack_y",
        limit=8 * 2**20,
    )(st, ld, active)
    ya, yb = exchange(ya, yb, "gy")
    sq = ((256, 256), bf16)
    *mats, inv0, listed = call(
        build_kernel,
        [
            ((256, 512), bf16), ((256, 512), bf16), ((64, 256), bf16), ((64, 256), bf16),
            sq, sq, sq, sq,
            sq, ((128, 256), bf16), ((128, 256), bf16),
            ((256, 256), f32), ((2, 256, 256), bf16), ((2, 256, 256), bf16),
            ((16, 128), bf16), ((16, 128), bf16), ((128, 16), bf16), ((128, 16), bf16),
            ((PATCH, 256, 256), bf16), ((16, 128), jnp.int32),
        ],
        [VMEM] + [ANY] * 6,
        [
            pltpu.SMEM((3, 5), f32),
            pltpu.SMEM((3, 5), f32),
            pltpu.VMEM((3, 16, 16), f32),
            pltpu.VMEM((3, 16), f32),
            pltpu.SMEM((2,), jnp.int32),
            dma((6,)),
        ],
        name="build",
    )(ac, stiff, mass, basis, values, cols_in, inverse)
    yh, yl, lh, ll, ayh, ayl, ath, atl, khl, kth, ktl, dinv, *cutters = mats
    sw, lw, aw, xa, xb = call(
        pack_x_kernel,
        [((256, 256), f32), ((256, 256), f32), ((32, 256), f32), ((120, 128), f32), ((120, 128), f32)],
        [VMEM] * 6,
        name="pack_x",
    )(lh, s, l, ac, ya, yb)
    inner_outs = [
        ((256, 512), bf16), ((256, 512), bf16),
        ((320, 256), bf16), ((320, 256), bf16), ((192, 256), bf16), ((192, 256), bf16),
        ((192, 256), f32), ((PATCH, 256, 256), bf16),
    ]
    inner_args = (sw, lw, aw, yh, yl, lh, ll, ayh, ayl, khl, kth, ktl, dinv, listed, inverse)
    *early, xb = call(
        inner_early_kernel,
        inner_outs + [((120, 128), f32)],
        [VMEM] * 14 + [ANY, VMEM],
        [dma],
        name="inner_early",
    )(*inner_args, xb)
    xa, xb = exchange(xa, xb, "gx")
    syh, syl, rh, rl, ryh, ryl, tin, inv1 = call(
        inner_kernel,
        inner_outs,
        [VMEM] * 14 + [ANY] + [VMEM] * 8,
        [dma],
        name="inner",
        aliases={15 + n: n for n in range(8)},
    )(*inner_args, *early)
    first, last, cut, xa, xb = call(
        edge_kernel,
        [
            ((96, 256), f32), ((96, 256), f32), ((320, 256), f32),
            ((48, 128), f32), ((48, 128), f32),
        ],
        [ANY] + [VMEM] * 31,
        [
            pltpu.VMEM((320, 256), bf16),
            pltpu.VMEM((320, 256), bf16),
            pltpu.SMEM((2,), jnp.int32),
            dma,
        ],
        name="edge",
    )(
        cols_in, lw, aw, xa, xb, syh, syl, rh, rl, ryh, ryl, inv0, inv1, listed,
        yh, yl, lh, ll, ayh, ayl, ath, atl, khl, kth, ktl, dinv, *cutters,
    )
    xa, xb = exchange(xa, xb, "gx")
    core, side = call(
        spread_kernel,
        [((256, 128), f32), ((16, 256), f32)],
        [ANY] + [VMEM] * 16,
        [pltpu.VMEM((320, 256), f32), pltpu.SMEM((2,), jnp.int32), dma],
        name="spread",
    )(cols_in, first, last, tin, cut, ath, atl, rh, rl, inv0, inv1, *cutters)
    ya, yb = call(
        join_x_kernel, [((8, 256), f32), ((8, 256), f32)], [VMEM] * 3, name="join_x"
    )(side, xa, xb)
    ya, yb = exchange(ya, yb, "gy")
    (out,) = call(finish_kernel, [((256, 128), f32)], [VMEM] * 7, name="finish")(
        core, xa, xb, ya, yb, s, ac
    )
    return out.reshape(8, 32, 128)


def solution(mesh):
    placed = (
        P(None, "gx", "gy"),
        P(None, "gx", "gy"),
        P("gx", "gy"),
        P(),
        P(),
        P(),
        P(),
        P("gx", "gy", None),
        P("gx", "gy", None, None, None, None),
    )
    return jax.shard_map(
        on_device, mesh=mesh, in_specs=placed, out_specs=P(None, "gx", "gy"), check_vma=False
    )
```

```python
import jax
import jax.numpy as jnp
from jax import lax
from jax.experimental import pallas as pl
from jax.experimental.pallas import tpu as pltpu
from jax.sharding import PartitionSpec as P

BAND = 4
PATCH = 16
damping = 0.5
FAR = 100000

f32 = jnp.float32
bf16 = jnp.bfloat16
VMEM = pl.BlockSpec(memory_space=pltpu.VMEM)
ANY = pl.BlockSpec(memory_space=pl.ANY)


def split(x):
    hi = x.astype(bf16)
    return hi, (x - hi.astype(f32)).astype(bf16)


def split3(x):
    hi, rest = x.astype(bf16), x
    rest = rest - hi.astype(f32)
    mid = rest.astype(bf16)
    return hi, mid, (rest - mid.astype(f32)).astype(bf16)


def dot(a, b):
    return lax.dot_general(a, b, (((1,), (0,)), ((), ())), preferred_element_type=f32)


def dot_t(a, b):
    return lax.dot_general(a, b, (((1,), (1,)), ((), ())), preferred_element_type=f32)


def dot3(ah, al, bh, bl):
    return dot(ah, bh) + (dot(ah, bl) + dot(al, bh))


def pick(x, onehot):
    h, m, l = split3(x)
    return dot(h, onehot) + dot(m, onehot) + dot(l, onehot)


def place(onehot, x):
    h, m, l = split3(x)
    return dot(onehot, h) + dot(onehot, m) + dot(onehot, l)


def iota(shape, dim):
    return lax.broadcasted_iota(jnp.int32, shape, dim)


def parity(axis):
    return lax.rem(lax.axis_index(axis), 2)


def y_coord(lane, par):
    far = lane * 64 + FAR
    above, below = lane, lane - 136
    first = jnp.where(par == 0, above, below)
    second = jnp.where(par == 0, below - 8, above - 8)
    return jnp.where(
        lane < 128, lane, jnp.where(lane < 136, first, jnp.where(lane < 144, second, far))
    )


def toeplitz(dist, coeffs):
    out = jnp.zeros(dist.shape, f32)
    for k in range(BAND + 1):
        out = jnp.where(dist == k, coeffs[k], out)
    return out


def fetch(pairs, sem):
    copies = [pltpu.make_async_copy(a, b, sem.at[n]) for n, (a, b) in enumerate(pairs)]
    for copy in copies:
        copy.start()
    for copy in copies:
        copy.wait()


def either(flag, a, b):
    return jnp.where(flag == 0, a, b)


def pack_y_kernel(
    st_hbm, ld_hbm, ac_hbm, s_out, l_out, a_out, send_a, send_b, st, ld, ac, wide, sem
):
    fetch([(st_hbm, st), (ld_hbm, ld), (ac_hbm, ac)], sem)
    py = parity("gy")
    wide[...] = ld[...].astype(f32)
    for x in range(32):
        s_out[8 * x : 8 * x + 8, :] = st[pl.ds(x, 8, stride=32), :]
        l_out[8 * x : 8 * x + 8, :] = wide[pl.ds(x, 8, stride=32), :]
    act = ac[...].astype(f32)
    a_out[...] = act
    turned = [s_out[...].T, l_out[...].T, jnp.concatenate([act, jnp.zeros((96, 128), f32)], axis=0).T]
    low = jnp.concatenate([t[0:8] for t in turned], axis=1)
    high = jnp.concatenate([t[120:128] for t in turned], axis=1)
    send_a[...] = either(py, high, low)
    send_b[...] = either(py, low, high)


def pack_x_kernel(after, s, l, ac, *refs):
    del after
    ra, rb = refs[0], refs[1]
    sw, lw, aw, send_a, send_b = refs[-5:]
    px = parity("gx")

    def strips(lanes, width):
        both = [ra[:, lanes], rb[:, lanes], jnp.zeros((112, width), f32)]
        return jnp.concatenate(both, axis=0).T

    sw[:, 0:128] = s[...]
    sw[:, 128:256] = strips(slice(0, 256), 256)
    lw[:, 0:128] = l[...]
    lw[:, 128:256] = strips(slice(256, 512), 256)
    aw[:, 0:128] = ac[...]
    aw[:, 128:256] = strips(slice(512, 640), 128)[0:32]

    def edge(srow, lrow, arow):
        rows = [sw[srow : srow + 64, :], lw[lrow : lrow + 32, :], aw[arow : arow + 8, :]]
        rows = jnp.concatenate(rows, axis=0)
        corner = jnp.concatenate([rows[:, 128:256], jnp.zeros((24, 128), f32)], axis=0).T
        return jnp.concatenate([rows[:, 0:128], corner[0:16]], axis=0)

    low, high = edge(0, 0, 0), edge(192, 224, 24)
    send_a[...] = either(px, high, low)
    send_b[...] = either(px, low, high)


def stencil(left_h, left_l, syh, syl, live, load):
    bh = jnp.concatenate([syh[:, 0:256], syh[:, 256:512]], axis=0)
    bl = jnp.concatenate([syl[:, 0:256], syl[:, 256:512]], axis=0)
    return split(live * (load - dot3(left_h, left_l, bh, bl)))


def solve_row(a, khl, kth, ktl, dinv, listed, ryh, ryl):
    modes = dot(khl, jnp.concatenate([ryh, ryh], axis=0)) + dot(khl[:, 0:128], ryl)
    lane_b = iota((1, 256), 1) >> 4
    keep = jnp.ones((1, 256), f32)
    for m in range(2):
        entry = jnp.concatenate([listed[8 * m : 8 * m + 1]] * 2, axis=1)
        keep = jnp.where(lane_b + 16 * a == entry, 0.0, keep)
    mh, ml = split(modes * dinv * keep)
    return dot3(kth, ktl, mh, ml)


def cut_values(ms, cols, rh, rl, sel, sel_t, lzh, lzl, lzth, lztl, invs):
    same = (iota((128, 256), 0) >> 3) == (iota((128, 256), 1) >> 4)
    lane_k = iota((256, 16), 1)
    rows = [pl.ds(pl.multiple_of(64 * (cols[m] >> 4), 64), 128) for m in ms]
    cells = [dot(rh[r, :], sel[m]) + dot(rl[r, :], sel[m]) for m, r in zip(ms, rows)]
    cells = [split(jnp.where(same, c, 0.0)) for c in cells]
    zmodes = [dot3(lzh[...], lzl[...], ch, cl).astype(bf16) for ch, cl in cells]
    wide = [z.astype(f32) for z in zmodes]
    dense = [jnp.zeros((256, 16), f32) for m in ms]
    for k in range(16):
        for n, m in enumerate(ms):
            if k % 2:
                terms = invs[m][k].astype(f32) * wide[n][k : k + 1]
                column = jnp.sum(terms, axis=1, keepdims=True)
            else:
                column = dot_t(invs[m][k], zmodes[n])
            dense[n] = jnp.where(lane_k == k, column, dense[n])
    out = []
    for m, r, d in zip(ms, rows, dense):
        dh, dl = split(d)
        back = dot_t(lzth[...], dh) + (dot_t(lzth[...], dl) + dot_t(lztl[...], dh))
        gh, gl = split(jnp.where(same, back, 0.0))
        out.append((r, dot(gh, sel_t[m]) + dot(gl, sel_t[m])))
    return out


def by_case(cols, places, body):
    need = []
    for m in range(2):
        a = cols[m] >> 4
        need.append((a == places[0]) | (a == places[1]))
    for ms in ((), (0,), (1,), (0, 1)):
        wanted = [need[m] if m in ms else jnp.logical_not(need[m]) for m in range(2)]
        pl.when(wanted[0] & wanted[1])(lambda ms=ms: body(ms))


def inner_kernel(
    sw, lw, aw, yh, yl, lh, ll, ayh, ayl, khl, kth, ktl, dinv, listed, inverse,
    syh, syl, rh, rl, ryh, ryl, tin, inv, sem,
):
    bulk = pltpu.make_async_copy(inverse.at[1], inv, sem)
    bulk.start()
    sh, sl = split(sw[...])
    syh[...], syl[...] = split(dot3(sh, sl, yh[...], yl[...]))
    spread = jnp.where((iota((192, 32), 0) >> 3) + 4 == iota((192, 32), 1), 1.0, 0.0)
    live = dot(spread.astype(bf16), aw[...].astype(bf16))
    rh[0:64, :] = jnp.zeros((64, 256), bf16)
    rl[0:64, :] = jnp.zeros((64, 256), bf16)
    rh[256:320, :] = jnp.zeros((64, 256), bf16)
    rl[256:320, :] = jnp.zeros((64, 256), bf16)
    for o in range(3):
        rows, mine = slice(64 * o, 64 * o + 128), slice(64 * o, 64 * o + 64)
        load = lw[64 * o + 32 : 64 * o + 96, :]
        into = slice(64 * o + 64, 64 * o + 128)
        rh[into, :], rl[into, :] = stencil(
            lh[...], ll[...], syh[rows, :], syl[rows, :], live[mine], load
        )
    ryh[...], ryl[...] = split(dot3(rh[64:256, :], rl[64:256, :], ayh[...], ayl[...]))
    rest = (khl[...], kth[...], ktl[...], dinv[...], listed[...])
    one = solve_row(1, *rest, ryh[0:128, :], ryl[0:128, :])
    two = solve_row(2, *rest, ryh[64:192, :], ryl[64:192, :])
    tin[0:64, :] = one[0:64]
    tin[64:128, :] = one[64:128] + two[0:64]
    tin[128:192, :] = two[64:128]
    bulk.wait()


def edge_kernel(
    lw, aw, syh, syl, rh_in, rl_in, ryh, ryl, inv0, inv1, listed,
    yh, yl, lh, ll, ayh, ayl, ath, atl, khl, kth, ktl, dinv, sel, sel_t, lzh, lzl, lzth, lztl,
    *refs,
):
    ra, rb = refs[0][...], refs[1][...]
    first, last, cut, send_a, send_b, rh, rl = refs[-7:]
    cols = [listed[8 * m, 0] for m in range(2)]
    px = parity("gx")
    low, high = either(px, rb, ra), either(px, ra, rb)

    def halo(block):
        corner = jnp.concatenate([block[104:120], jnp.zeros((112, 128), f32)], axis=0).T
        return jnp.concatenate([block[0:104], corner[0:104]], axis=1)

    low, high = halo(low), halo(high)
    sh, sl = split(jnp.concatenate([low[0:64], high[0:64]], axis=0))
    ehh, ehl = split(dot3(sh, sl, yh[...], yl[...]))
    spread = jnp.where((iota((64, 16), 0) >> 3) + 4 == iota((64, 16), 1), 1.0, 0.0).astype(bf16)
    rh[64:256, :], rl[64:256, :] = rh_in[64:256, :], rl_in[64:256, :]
    live = dot(spread, jnp.concatenate([low[96:104], aw[0:8, :]], axis=0).astype(bf16))
    rh[0:64, :], rl[0:64, :] = stencil(
        lh[...],
        ll[...],
        jnp.concatenate([ehh[0:64], syh[0:64, :]], axis=0),
        jnp.concatenate([ehl[0:64], syl[0:64, :]], axis=0),
        live,
        jnp.concatenate([low[64:96], lw[0:32, :]], axis=0),
    )
    live = dot(spread, jnp.concatenate([aw[24:32, :], high[96:104]], axis=0).astype(bf16))
    rh[256:320, :], rl[256:320, :] = stencil(
        lh[...],
        ll[...],
        jnp.concatenate([syh[192:256, :], ehh[64:128]], axis=0),
        jnp.concatenate([syl[192:256, :], ehl[64:128]], axis=0),
        live,
        jnp.concatenate([lw[224:256, :], high[64:96]], axis=0),
    )
    cut[...] = jnp.zeros((320, 256), f32)

    def tail(ms):
        args = (rh, rl, sel, sel_t, lzh, lzl, lzth, lztl, (inv0, inv1))
        values = cut_values(ms, cols, *args)
        edges_h = jnp.concatenate([rh[0:64, :], rh[256:320, :]], axis=0)
        edges_l = jnp.concatenate([rl[0:64, :], rl[256:320, :]], axis=0)
        eyh, eyl = split(dot3(edges_h, edges_l, ayh[...], ayl[...]))
        rest = (khl[...], kth[...], ktl[...], dinv[...], listed[...])
        t0 = solve_row(
            0,
            *rest,
            jnp.concatenate([eyh[0:64], ryh[0:64, :]], axis=0),
            jnp.concatenate([eyl[0:64], ryl[0:64, :]], axis=0),
        )
        t3 = solve_row(
            3,
            *rest,
            jnp.concatenate([ryh[128:192, :], eyh[64:128]], axis=0),
            jnp.concatenate([ryl[128:192, :], eyl[64:128]], axis=0),
        )
        first[...], last[...] = t0[32:128], t3[0:96]
        th, tl = split(jnp.concatenate([t0[0:32], t3[96:128]], axis=0))
        out = dot3(th, tl, ath[...], atl[...])
        for rows, value in values:
            cut[rows, :] += value
        out_low, out_high = out[0:32] + cut[0:32, :], out[32:64] + cut[288:320, :]
        pad = jnp.zeros((96, 128), f32)
        corner_low = jnp.concatenate([pad, out_low[:, 128:256]], axis=0).T
        corner_high = jnp.concatenate([out_high[:, 128:256], pad], axis=0).T
        out_low = jnp.concatenate([out_low[:, 0:128], corner_low[0:16]], axis=0)
        out_high = jnp.concatenate([out_high[:, 0:128], corner_high[0:16]], axis=0)
        send_a[...] = either(px, out_high, out_low)
        send_b[...] = either(px, out_low, out_high)

    by_case(cols, (0, 3), tail)


def spread_kernel(
    listed, first, last, tin, cut_in, ath, atl, rh, rl, inv0, inv1,
    sel, sel_t, lzh, lzl, lzth, lztl, core, side, cut,
):
    cols = [listed[8 * m, 0] for m in range(2)]
    cut[...] = cut_in[...]

    def body(ms):
        args = (rh, rl, sel, sel_t, lzh, lzl, lzth, lztl, (inv0, inv1))
        values = cut_values(ms, cols, *args)
        total = jnp.concatenate(
            [
                first[0:32, :],
                first[32:96, :] + tin[0:64, :],
                tin[64:128, :],
                tin[128:192, :] + last[0:64, :],
                last[64:96, :],
            ],
            axis=0,
        )
        th, tl = split(total)
        total = dot3(th, tl, ath[...], atl[...])
        for rows, value in values:
            cut[rows, :] += value
        total = total + cut[32:288, :]
        core[...] = total[:, 0:128]
        side[...] = total[:, 128:256].T[0:16]

    by_case(cols, (1, 2), body)


def join_x_kernel(side, *refs):
    px = parity("gx")
    ra, rb = refs[0], refs[1]
    send_a, send_b = refs[-2:]
    low, high = either(px, rb[32:48, :], ra[32:48, :]), either(px, ra[32:48, :], rb[32:48, :])
    full = side[...] + jnp.concatenate([low, high], axis=1)
    send_a[...] = full[0:8]
    send_b[...] = full[8:16]


def finish_kernel(core, s, ac, xa, xb, ya, yb, out):
    px, py = parity("gx"), parity("gy")
    low, high = either(px, xb[0:32, :], xa[0:32, :]), either(px, xa[0:32, :], xb[0:32, :])
    left, right = either(py, yb[...], ya[...]), either(py, ya[...], yb[...])
    edge = jnp.concatenate([left, jnp.zeros((112, 256), f32), right], axis=0).T
    total = core[...] + edge
    for x in range(32):
        term = total[8 * x : 8 * x + 8]
        if x < 4:
            term = term + low[8 * x : 8 * x + 8]
        if x >= 28:
            term = term + high[8 * (x - 28) : 8 * (x - 28) + 8]
        row = damping * ac[pl.ds(x, 1), :]
        out[pl.ds(x, 8, stride=32), :] = s[8 * x : 8 * x + 8, :] + row * term


def build_kernel(
    after, stiff_hbm, mass_hbm, basis_hbm, values_hbm, cols_hbm, inverse,
    yh, yl, lh, ll, ayh, ayl, ath, atl, khl, kth, ktl, dinv, sel, sel_t, lzh, lzl, lzth, lztl, inv, listed,
    stiff, mass, basis, values, cols, sem,
):
    del after
    bulk = pltpu.make_async_copy(inverse.at[0], inv, sem.at[5])
    bulk.start()
    fetch(
        [
            (stiff_hbm, stiff),
            (mass_hbm, mass),
            (basis_hbm, basis),
            (values_hbm, values),
            (cols_hbm, cols),
        ],
        sem,
    )
    py = parity("gy")
    kz, kx, ky = ([stiff[d, k] for k in range(BAND + 1)] for d in range(3))
    mz, mx, my = ([mass[d, k] for k in range(BAND + 1)] for d in range(3))
    dist = jnp.abs(y_coord(iota((256, 256), 0), py) - y_coord(iota((256, 256), 1), py))
    yh[:, 0:256], yl[:, 0:256] = split(toeplitz(dist, my))
    yh[:, 256:512], yl[:, 256:512] = split(toeplitz(dist, ky))
    row, col = iota((64, 128), 0), iota((64, 128), 1)
    dx = jnp.abs((row >> 3) + 4 - (col >> 3))
    dz = jnp.abs((row & 7) - (col & 7))
    tmz, tmx = toeplitz(dz, mz), toeplitz(dx, mx)
    first = tmz * toeplitz(dx, kx) + toeplitz(dz, kz) * tmx
    lh[:, 0:128], ll[:, 0:128] = split(first)
    lh[:, 128:256], ll[:, 128:256] = split(tmz * tmx)
    one = lambda cond: jnp.where(cond, 1.0, 0.0).astype(bf16)
    tile_j = one(iota((16, 256), 0) == (iota((16, 256), 1) & 15))
    vy = pick(basis[2], tile_j)
    c = y_coord(iota((256, 256), 0), py)
    b = iota((256, 256), 1) >> 4
    t = c + 4 - 8 * b
    lower = jnp.concatenate([vy[4:8], vy[0:4]], axis=0)
    upper = jnp.concatenate([vy[12:16], vy[8:12]], axis=0)
    lower = jnp.concatenate([lower] * 32, axis=0)
    upper = jnp.concatenate([upper] * 32, axis=0)
    ay = jnp.where((t >= 0) & (t < 8), lower, jnp.where((t >= 8) & (t < 16), upper, 0.0))
    ayh[...], ayl[...] = split(ay)
    ath[...], atl[...] = split(ay.T)
    to_i = one((iota((256, 16), 0) >> 4) == iota((256, 16), 1))
    to_k = one((iota((256, 16), 0) & 15) == iota((256, 16), 1))
    to_xx = one((iota((16, 128), 1) >> 3) == iota((16, 128), 0))
    to_z = one((iota((16, 128), 1) & 7) + 4 == iota((16, 128), 0))
    vz_rows = pick(basis[0].T, to_z)
    vx_rows = pick(basis[1].T, to_xx)
    kron = place(to_i, vx_rows) * place(to_k, vz_rows)
    khl[:, 0:128], khl[:, 128:256] = split(kron)
    kth[...], ktl[...] = split(kron.T)
    lzh[...], lzl[...] = split(vz_rows)
    lzth[...], lztl[...] = split(vz_rows.T)
    lam = values[...]
    lanes = pick(jnp.concatenate([lam, jnp.zeros((5, 16), f32)], axis=0), tile_j)[2:3]
    lam_t = jnp.concatenate([lam, jnp.zeros((5, 16), f32)], axis=0).T
    lam_i, lam_k = place(to_i, lam_t)[:, 1:2], place(to_k, lam_t)[:, 0:1]
    dinv[...] = 1.0 / (lam_k + lam_i + lanes)
    yy = iota((256, 256), 1) & 15
    cy = y_coord(iota((256, 256), 0), py)
    yy_t = iota((256, 256), 0) & 15
    cy_t = y_coord(iota((256, 256), 1), py)
    for m in range(2):
        entry = cols[m]
        at = jnp.where(entry >= 0, 8 * (jnp.maximum(entry, 0) & 15) - 4, -4 * FAR)
        sel[m] = one(cy == yy + at)
        sel_t[m] = one(cy_t == yy_t + at)
        listed[8 * m : 8 * m + 8, :] = jnp.full((8, 128), entry, jnp.int32)
    bulk.wait()


def call(kernel, outs, ins, scratch=(), name=None, aliases=None, limit=8 * 2**20):
    return pl.pallas_call(
        kernel,
        out_shape=[jax.ShapeDtypeStruct(s, t) for s, t in outs],
        in_specs=ins,
        out_specs=[VMEM] * len(outs),
        scratch_shapes=scratch,
        name=name,
        compiler_params=pltpu.CompilerParams(vmem_limit_bytes=limit),
        input_output_aliases=aliases or {},
        cost_estimate=pl.CostEstimate(flops=10**6, bytes_accessed=10**6, transcendentals=0),
    )


def swaps(axis, first):
    size = lax.axis_size(axis)
    lows = range(first, size - 1, 2)
    return [(i, i + 1) for i in lows] + [(i + 1, i) for i in lows]


def exchange(a, b, axis):
    return lax.ppermute(a, axis, swaps(axis, 0)), lax.ppermute(b, axis, swaps(axis, 1))


def on_device(
    state, load_vector, active, stiff_band, mass_band, eig_basis, eig_values, cut_cols, cut_inverse
):
    st, ld, active, stiff, mass, basis, values, cols_in, inverse = (
        pltpu.with_memory_space_constraint(x, pltpu.HBM)
        for x in (
            state.reshape(256, 128),
            load_vector.reshape(256, 128),
            active,
            stiff_band,
            mass_band,
            eig_basis,
            eig_values,
            cut_cols.reshape(2),
            cut_inverse.reshape(2, PATCH, 256, 256),
        )
    )
    dma = pltpu.SemaphoreType.DMA
    s, l, ac, ya, yb = call(
        pack_y_kernel,
        [((256, 128), f32), ((256, 128), f32), ((32, 128), f32), ((8, 640), f32), ((8, 640), f32)],
        [ANY] * 3,
        [
            pltpu.VMEM((256, 128), f32),
            pltpu.VMEM((256, 128), bf16),
            pltpu.VMEM((32, 128), jnp.int32),
            pltpu.VMEM((256, 128), f32),
            dma((3,)),
        ],
        name="pack_y",
        limit=8 * 2**20,
    )(st, ld, active)
    ys = exchange(ya, yb, "gy")
    sq = ((256, 256), bf16)
    *mats, inv0, listed = call(
        build_kernel,
        [
            ((256, 512), bf16), ((256, 512), bf16), ((64, 256), bf16), ((64, 256), bf16),
            sq, sq, sq, sq,
            sq, ((128, 256), bf16), ((128, 256), bf16),
            ((256, 256), f32), ((2, 256, 256), bf16), ((2, 256, 256), bf16),
            ((16, 128), bf16), ((16, 128), bf16), ((128, 16), bf16), ((128, 16), bf16),
            ((PATCH, 256, 256), bf16), ((16, 128), jnp.int32),
        ],
        [VMEM] + [ANY] * 6,
        [
            pltpu.SMEM((3, 5), f32),
            pltpu.SMEM((3, 5), f32),
            pltpu.VMEM((3, 16, 16), f32),
            pltpu.VMEM((3, 16), f32),
            pltpu.SMEM((2,), jnp.int32),
            dma((6,)),
        ],
        name="build",
    )(ac, stiff, mass, basis, values, cols_in, inverse)
    yh, yl, lh, ll, ayh, ayl, ath, atl, khl, kth, ktl, dinv, *cutters = mats
    sw, lw, aw, xa, xb = call(
        pack_x_kernel,
        [((256, 256), f32), ((256, 256), f32), ((32, 256), f32), ((120, 128), f32), ((120, 128), f32)],
        [VMEM] * (4 + len(ys)),
        name="pack_x",
    )(lh, s, l, ac, *ys)
    inner_outs = [
        ((256, 512), bf16), ((256, 512), bf16),
        ((320, 256), bf16), ((320, 256), bf16), ((192, 256), bf16), ((192, 256), bf16),
        ((192, 256), f32), ((PATCH, 256, 256), bf16),
    ]
    inner_args = (sw, lw, aw, yh, yl, lh, ll, ayh, ayl, khl, kth, ktl, dinv, listed, inverse)
    xs = exchange(xa, xb, "gx")
    syh, syl, rh, rl, ryh, ryl, tin, inv1 = call(
        inner_kernel, inner_outs, [VMEM] * 14 + [ANY], [dma], name="inner"
    )(*inner_args)
    first, last, cut, xa, xb = call(
        edge_kernel,
        [
            ((96, 256), f32), ((96, 256), f32), ((320, 256), f32),
            ((48, 128), f32), ((48, 128), f32),
        ],
        [VMEM] * (29 + len(xs)),
        [pltpu.VMEM((320, 256), bf16), pltpu.VMEM((320, 256), bf16)],
        name="edge",
    )(
        lw, aw, syh, syl, rh, rl, ryh, ryl, inv0, inv1, listed,
        yh, yl, lh, ll, ayh, ayl, ath, atl, khl, kth, ktl, dinv, *cutters, *xs,
    )
    xs = exchange(xa, xb, "gx")
    core, side = call(
        spread_kernel,
        [((256, 128), f32), ((16, 256), f32)],
        [VMEM] * 17,
        [pltpu.VMEM((320, 256), f32)],
        name="spread",
    )(listed, first, last, tin, cut, ath, atl, rh, rl, inv0, inv1, *cutters)
    ya, yb = call(
        join_x_kernel, [((8, 256), f32), ((8, 256), f32)], [VMEM] * (1 + len(xs)), name="join_x"
    )(side, *xs)
    ys = exchange(ya, yb, "gy")
    (out,) = call(finish_kernel, [((256, 128), f32)], [VMEM] * 7, name="finish")(
        core, s, ac, *xs, *ys
    )
    return out.reshape(8, 32, 128)


def solution(mesh):
    placed = (
        P(None, "gx", "gy"),
        P(None, "gx", "gy"),
        P("gx", "gy"),
        P(),
        P(),
        P(),
        P(),
        P("gx", "gy", None),
        P("gx", "gy", None, None, None, None),
    )
    return jax.shard_map(
        on_device, mesh=mesh, in_specs=placed, out_specs=P(None, "gx", "gy"), check_vma=False
    )
```

```python
import jax
import jax.numpy as jnp
from jax import lax
from jax.experimental import pallas as pl
from jax.experimental.pallas import tpu as pltpu
from jax.sharding import PartitionSpec as P

BAND = 4
PATCH = 16
damping = 0.5
FAR = 100000

f32 = jnp.float32
bf16 = jnp.bfloat16
VMEM = pl.BlockSpec(memory_space=pltpu.VMEM)
ANY = pl.BlockSpec(memory_space=pl.ANY)


def split(x):
    hi = x.astype(bf16)
    return hi, (x - hi.astype(f32)).astype(bf16)


def split3(x):
    hi, rest = x.astype(bf16), x
    rest = rest - hi.astype(f32)
    mid = rest.astype(bf16)
    return hi, mid, (rest - mid.astype(f32)).astype(bf16)


def dot(a, b):
    return lax.dot_general(a, b, (((1,), (0,)), ((), ())), preferred_element_type=f32)


def dot_t(a, b):
    return lax.dot_general(a, b, (((1,), (1,)), ((), ())), preferred_element_type=f32)


def dot3(ah, al, bh, bl):
    return dot(ah, bh) + (dot(ah, bl) + dot(al, bh))


def pick(x, onehot):
    h, m, l = split3(x)
    return dot(h, onehot) + dot(m, onehot) + dot(l, onehot)


def place(onehot, x):
    h, m, l = split3(x)
    return dot(onehot, h) + dot(onehot, m) + dot(onehot, l)


def iota(shape, dim):
    return lax.broadcasted_iota(jnp.int32, shape, dim)


def parity(axis):
    return lax.rem(lax.axis_index(axis), 2)


def y_coord(lane, par):
    far = lane * 64 + FAR
    above, below = lane, lane - 136
    first = jnp.where(par == 0, above, below)
    second = jnp.where(par == 0, below - 8, above - 8)
    return jnp.where(
        lane < 128, lane, jnp.where(lane < 136, first, jnp.where(lane < 144, second, far))
    )


def toeplitz(dist, coeffs):
    out = jnp.zeros(dist.shape, f32)
    for k in range(BAND + 1):
        out = jnp.where(dist == k, coeffs[k], out)
    return out


def either(flag, a, b):
    return jnp.where(flag == 0, a, b)


def pack_y_kernel(
    st_hbm, ld_hbm, ac_hbm, s_out, l_out, a_out, send_a, send_b, st, ld, ac, wide, sem
):
    pairs = [(st_hbm, st), (ld_hbm, ld), (ac_hbm, ac)]
    copies = [pltpu.make_async_copy(a, b, sem.at[n]) for n, (a, b) in enumerate(pairs)]
    for copy in copies:
        copy.start()
    py = parity("gy")
    for copy in copies:
        copy.wait()
    wide[...] = ld[...].astype(f32)
    for x in range(32):
        s_out[8 * x : 8 * x + 8, :] = st[pl.ds(x, 8, stride=32), :]
        l_out[8 * x : 8 * x + 8, :] = wide[pl.ds(x, 8, stride=32), :]
    act = ac[...].astype(f32)
    a_out[...] = act
    turned = [s_out[...].T, l_out[...].T, jnp.concatenate([act, jnp.zeros((96, 128), f32)], axis=0).T]
    low = jnp.concatenate([t[0:8] for t in turned], axis=1)
    high = jnp.concatenate([t[120:128] for t in turned], axis=1)
    send_a[...] = either(py, high, low)
    send_b[...] = either(py, low, high)


def pack_x_kernel(after, s, l, ac, *refs):
    del after
    ra, rb = refs[0], refs[1]
    sw, lw, aw, send_a, send_b = refs[-5:]
    px = parity("gx")

    def strips(lanes, width):
        both = [ra[:, lanes], rb[:, lanes], jnp.zeros((112, width), f32)]
        return jnp.concatenate(both, axis=0).T

    sw[:, 0:128] = s[...]
    sw[:, 128:256] = strips(slice(0, 256), 256)
    lw[:, 0:128] = l[...]
    lw[:, 128:256] = strips(slice(256, 512), 256)
    aw[:, 0:128] = ac[...]
    aw[:, 128:256] = strips(slice(512, 640), 128)[0:32]

    def edge(srow, lrow, arow):
        rows = [sw[srow : srow + 64, :], lw[lrow : lrow + 32, :], aw[arow : arow + 8, :]]
        rows = jnp.concatenate(rows, axis=0)
        corner = jnp.concatenate([rows[:, 128:256], jnp.zeros((24, 128), f32)], axis=0).T
        return jnp.concatenate([rows[:, 0:128], corner[0:16]], axis=0)

    low, high = edge(0, 0, 0), edge(192, 224, 24)
    send_a[...] = either(px, high, low)
    send_b[...] = either(px, low, high)


def stencil(left_h, left_l, syh, syl, live, load):
    bh = jnp.concatenate([syh[:, 0:256], syh[:, 256:512]], axis=0)
    bl = jnp.concatenate([syl[:, 0:256], syl[:, 256:512]], axis=0)
    return split(live * (load - dot3(left_h, left_l, bh, bl)))


def solve_row(a, khl, kth, ktl, dinv, listed, ryh, ryl):
    modes = dot(khl, jnp.concatenate([ryh, ryh], axis=0)) + dot(khl[:, 0:128], ryl)
    lane_b = iota((1, 256), 1) >> 4
    keep = jnp.ones((1, 256), f32)
    for m in range(2):
        entry = jnp.concatenate([listed[8 * m : 8 * m + 1]] * 2, axis=1)
        keep = jnp.where(lane_b + 16 * a == entry, 0.0, keep)
    mh, ml = split(modes * dinv * keep)
    return dot3(kth, ktl, mh, ml)


def cut_values(ms, cols, rh, rl, sel, sel_t, lzh, lzl, lzth, lztl, invs):
    same = (iota((128, 256), 0) >> 3) == (iota((128, 256), 1) >> 4)
    lane_k = iota((256, 16), 1)
    rows = [pl.ds(pl.multiple_of(64 * (cols[m] >> 4), 64), 128) for m in ms]
    cells = [dot(rh[r, :], sel[m]) + dot(rl[r, :], sel[m]) for m, r in zip(ms, rows)]
    cells = [split(jnp.where(same, c, 0.0)) for c in cells]
    zmodes = [dot3(lzh[...], lzl[...], ch, cl).astype(bf16) for ch, cl in cells]
    wide = [z.astype(f32) for z in zmodes]
    dense = [jnp.zeros((256, 16), f32) for m in ms]
    for k in range(16):
        for n, m in enumerate(ms):
            if k % 2:
                terms = invs[m][k].astype(f32) * wide[n][k : k + 1]
                column = jnp.sum(terms, axis=1, keepdims=True)
            else:
                column = dot_t(invs[m][k], zmodes[n])
            dense[n] = jnp.where(lane_k == k, column, dense[n])
    out = []
    for m, r, d in zip(ms, rows, dense):
        dh, dl = split(d)
        back = dot_t(lzth[...], dh) + (dot_t(lzth[...], dl) + dot_t(lztl[...], dh))
        gh, gl = split(jnp.where(same, back, 0.0))
        out.append((r, dot(gh, sel_t[m]) + dot(gl, sel_t[m])))
    return out


def by_case(cols, places, body):
    need = []
    for m in range(2):
        a = cols[m] >> 4
        need.append((a == places[0]) | (a == places[1]))
    for ms in ((0, 1), (1,), (0,), ()):
        wanted = [need[m] if m in ms else jnp.logical_not(need[m]) for m in range(2)]
        pl.when(wanted[0] & wanted[1])(lambda ms=ms: body(ms))


def inner_kernel(
    sw, lw, aw, yh, yl, lh, ll, ayh, ayl, khl, kth, ktl, dinv, listed, inverse,
    syh, syl, rh, rl, ryh, ryl, tin, inv, sem,
):
    bulk = pltpu.make_async_copy(inverse.at[1], inv, sem)
    bulk.start()
    sh, sl = split(sw[...])
    syh[...], syl[...] = split(dot3(sh, sl, yh[...], yl[...]))
    spread = jnp.where((iota((192, 32), 0) >> 3) + 4 == iota((192, 32), 1), 1.0, 0.0)
    live = dot(spread.astype(bf16), aw[...].astype(bf16))
    rh[0:64, :] = jnp.zeros((64, 256), bf16)
    rl[0:64, :] = jnp.zeros((64, 256), bf16)
    rh[256:320, :] = jnp.zeros((64, 256), bf16)
    rl[256:320, :] = jnp.zeros((64, 256), bf16)
    for o in range(3):
        rows, mine = slice(64 * o, 64 * o + 128), slice(64 * o, 64 * o + 64)
        load = lw[64 * o + 32 : 64 * o + 96, :]
        into = slice(64 * o + 64, 64 * o + 128)
        rh[into, :], rl[into, :] = stencil(
            lh[...], ll[...], syh[rows, :], syl[rows, :], live[mine], load
        )
    ryh[...], ryl[...] = split(dot3(rh[64:256, :], rl[64:256, :], ayh[...], ayl[...]))
    rest = (khl[...], kth[...], ktl[...], dinv[...], listed[...])
    one = solve_row(1, *rest, ryh[0:128, :], ryl[0:128, :])
    two = solve_row(2, *rest, ryh[64:192, :], ryl[64:192, :])
    tin[0:64, :] = one[0:64]
    tin[64:128, :] = one[64:128] + two[0:64]
    tin[128:192, :] = two[64:128]
    bulk.wait()


def edge_kernel(
    lw, aw, syh, syl, rh_in, rl_in, ryh, ryl, inv0, inv1, listed,
    yh, yl, lh, ll, ayh, ayl, ath, atl, khl, kth, ktl, dinv, sel, sel_t, lzh, lzl, lzth, lztl,
    *refs,
):
    ra, rb = refs[0][...], refs[1][...]
    first, last, cut, send_a, send_b, rh, rl = refs[-7:]
    cols = [listed[8 * m, 0] for m in range(2)]
    px = parity("gx")
    low, high = either(px, rb, ra), either(px, ra, rb)

    def halo(block):
        corner = jnp.concatenate([block[104:120], jnp.zeros((112, 128), f32)], axis=0).T
        return jnp.concatenate([block[0:104], corner[0:104]], axis=1)

    low, high = halo(low), halo(high)
    sh, sl = split(jnp.concatenate([low[0:64], high[0:64]], axis=0))
    ehh, ehl = split(dot3(sh, sl, yh[...], yl[...]))
    spread = jnp.where((iota((64, 16), 0) >> 3) + 4 == iota((64, 16), 1), 1.0, 0.0).astype(bf16)
    rh[64:256, :], rl[64:256, :] = rh_in[64:256, :], rl_in[64:256, :]
    live = dot(spread, jnp.concatenate([low[96:104], aw[0:8, :]], axis=0).astype(bf16))
    rh[0:64, :], rl[0:64, :] = stencil(
        lh[...],
        ll[...],
        jnp.concatenate([ehh[0:64], syh[0:64, :]], axis=0),
        jnp.concatenate([ehl[0:64], syl[0:64, :]], axis=0),
        live,
        jnp.concatenate([low[64:96], lw[0:32, :]], axis=0),
    )
    live = dot(spread, jnp.concatenate([aw[24:32, :], high[96:104]], axis=0).astype(bf16))
    rh[256:320, :], rl[256:320, :] = stencil(
        lh[...],
        ll[...],
        jnp.concatenate([syh[192:256, :], ehh[64:128]], axis=0),
        jnp.concatenate([syl[192:256, :], ehl[64:128]], axis=0),
        live,
        jnp.concatenate([lw[224:256, :], high[64:96]], axis=0),
    )
    cut[...] = jnp.zeros((320, 256), f32)

    def tail(ms):
        args = (rh, rl, sel, sel_t, lzh, lzl, lzth, lztl, (inv0, inv1))
        values = cut_values(ms, cols, *args)
        edges_h = jnp.concatenate([rh[0:64, :], rh[256:320, :]], axis=0)
        edges_l = jnp.concatenate([rl[0:64, :], rl[256:320, :]], axis=0)
        eyh, eyl = split(dot3(edges_h, edges_l, ayh[...], ayl[...]))
        rest = (khl[...], kth[...], ktl[...], dinv[...], listed[...])
        t0 = solve_row(
            0,
            *rest,
            jnp.concatenate([eyh[0:64], ryh[0:64, :]], axis=0),
            jnp.concatenate([eyl[0:64], ryl[0:64, :]], axis=0),
        )
        t3 = solve_row(
            3,
            *rest,
            jnp.concatenate([ryh[128:192, :], eyh[64:128]], axis=0),
            jnp.concatenate([ryl[128:192, :], eyl[64:128]], axis=0),
        )
        first[...], last[...] = t0[32:128], t3[0:96]
        th, tl = split(jnp.concatenate([t0[0:32], t3[96:128]], axis=0))
        out = dot3(th, tl, ath[...], atl[...])
        for rows, value in values:
            cut[rows, :] += value
        out_low, out_high = out[0:32] + cut[0:32, :], out[32:64] + cut[288:320, :]
        pad = jnp.zeros((96, 128), f32)
        corner_low = jnp.concatenate([pad, out_low[:, 128:256]], axis=0).T
        corner_high = jnp.concatenate([out_high[:, 128:256], pad], axis=0).T
        out_low = jnp.concatenate([out_low[:, 0:128], corner_low[0:16]], axis=0)
        out_high = jnp.concatenate([out_high[:, 0:128], corner_high[0:16]], axis=0)
        send_a[...] = either(px, out_high, out_low)
        send_b[...] = either(px, out_low, out_high)

    by_case(cols, (0, 3), tail)


def spread_kernel(
    listed, first, last, tin, cut_in, ath, atl, rh, rl, inv0, inv1,
    sel, sel_t, lzh, lzl, lzth, lztl, core, side, cut,
):
    cols = [listed[8 * m, 0] for m in range(2)]
    cut[...] = cut_in[...]

    def body(ms):
        args = (rh, rl, sel, sel_t, lzh, lzl, lzth, lztl, (inv0, inv1))
        values = cut_values(ms, cols, *args)
        total = jnp.concatenate(
            [
                first[0:32, :],
                first[32:96, :] + tin[0:64, :],
                tin[64:128, :],
                tin[128:192, :] + last[0:64, :],
                last[64:96, :],
            ],
            axis=0,
        )
        th, tl = split(total)
        total = dot3(th, tl, ath[...], atl[...])
        for rows, value in values:
            cut[rows, :] += value
        total = total + cut[32:288, :]
        core[...] = total[:, 0:128]
        side[...] = total[:, 128:256].T[0:16]

    by_case(cols, (1, 2), body)


def join_x_kernel(side, *refs):
    px = parity("gx")
    ra, rb = refs[0], refs[1]
    send_a, send_b = refs[-2:]
    low, high = either(px, rb[32:48, :], ra[32:48, :]), either(px, ra[32:48, :], rb[32:48, :])
    full = side[...] + jnp.concatenate([low, high], axis=1)
    send_a[...] = full[0:8]
    send_b[...] = full[8:16]


def finish_kernel(core, s, ac, xa, xb, ya, yb, out):
    px, py = parity("gx"), parity("gy")
    low, high = either(px, xb[0:32, :], xa[0:32, :]), either(px, xa[0:32, :], xb[0:32, :])
    left, right = either(py, yb[...], ya[...]), either(py, ya[...], yb[...])
    edge = jnp.concatenate([left, jnp.zeros((112, 256), f32), right], axis=0).T
    total = core[...] + edge
    for x in range(32):
        term = total[8 * x : 8 * x + 8]
        if x < 4:
            term = term + low[8 * x : 8 * x + 8]
        if x >= 28:
            term = term + high[8 * (x - 28) : 8 * (x - 28) + 8]
        row = damping * ac[pl.ds(x, 1), :]
        out[pl.ds(x, 8, stride=32), :] = s[8 * x : 8 * x + 8, :] + row * term


def build_kernel(
    after, stiff_hbm, mass_hbm, basis_hbm, values_hbm, cols_hbm, inverse,
    yh, yl, lh, ll, ayh, ayl, ath, atl, khl, kth, ktl, dinv, sel, sel_t, lzh, lzl, lzth, lztl, inv, listed,
    stiff, mass, basis, values, cols, sem,
):
    del after
    pairs = [
        (stiff_hbm, stiff),
        (mass_hbm, mass),
        (basis_hbm, basis),
        (values_hbm, values),
        (cols_hbm, cols),
    ]
    small = [pltpu.make_async_copy(a, b, sem.at[n]) for n, (a, b) in enumerate(pairs)]
    bulk = pltpu.make_async_copy(inverse.at[0], inv, sem.at[5])
    for copy in small + [bulk]:
        copy.start()
    for copy in small:
        copy.wait()
    py = parity("gy")
    kz, kx, ky = ([stiff[d, k] for k in range(BAND + 1)] for d in range(3))
    mz, mx, my = ([mass[d, k] for k in range(BAND + 1)] for d in range(3))
    dist = jnp.abs(y_coord(iota((256, 256), 0), py) - y_coord(iota((256, 256), 1), py))
    yh[:, 0:256], yl[:, 0:256] = split(toeplitz(dist, my))
    yh[:, 256:512], yl[:, 256:512] = split(toeplitz(dist, ky))
    row, col = iota((64, 128), 0), iota((64, 128), 1)
    dx = jnp.abs((row >> 3) + 4 - (col >> 3))
    dz = jnp.abs((row & 7) - (col & 7))
    tmz, tmx = toeplitz(dz, mz), toeplitz(dx, mx)
    first = tmz * toeplitz(dx, kx) + toeplitz(dz, kz) * tmx
    lh[:, 0:128], ll[:, 0:128] = split(first)
    lh[:, 128:256], ll[:, 128:256] = split(tmz * tmx)
    one = lambda cond: jnp.where(cond, 1.0, 0.0).astype(bf16)
    tile_j = one(iota((16, 256), 0) == (iota((16, 256), 1) & 15))
    vy = pick(basis[2], tile_j)
    c = y_coord(iota((256, 256), 0), py)
    b = iota((256, 256), 1) >> 4
    t = c + 4 - 8 * b
    lower = jnp.concatenate([vy[4:8], vy[0:4]], axis=0)
    upper = jnp.concatenate([vy[12:16], vy[8:12]], axis=0)
    lower = jnp.concatenate([lower] * 32, axis=0)
    upper = jnp.concatenate([upper] * 32, axis=0)
    ay = jnp.where((t >= 0) & (t < 8), lower, jnp.where((t >= 8) & (t < 16), upper, 0.0))
    ayh[...], ayl[...] = split(ay)
    ath[...], atl[...] = split(ay.T)
    to_i = one((iota((256, 16), 0) >> 4) == iota((256, 16), 1))
    to_k = one((iota((256, 16), 0) & 15) == iota((256, 16), 1))
    to_xx = one((iota((16, 128), 1) >> 3) == iota((16, 128), 0))
    to_z = one((iota((16, 128), 1) & 7) + 4 == iota((16, 128), 0))
    vz_rows = pick(basis[0].T, to_z)
    vx_rows = pick(basis[1].T, to_xx)
    kron = place(to_i, vx_rows) * place(to_k, vz_rows)
    khl[:, 0:128], khl[:, 128:256] = split(kron)
    kth[...], ktl[...] = split(kron.T)
    lzh[...], lzl[...] = split(vz_rows)
    lzth[...], lztl[...] = split(vz_rows.T)
    lam = values[...]
    lanes = pick(jnp.concatenate([lam, jnp.zeros((5, 16), f32)], axis=0), tile_j)[2:3]
    lam_t = jnp.concatenate([lam, jnp.zeros((5, 16), f32)], axis=0).T
    lam_i, lam_k = place(to_i, lam_t)[:, 1:2], place(to_k, lam_t)[:, 0:1]
    dinv[...] = 1.0 / (lam_k + lam_i + lanes)
    yy = iota((256, 256), 1) & 15
    cy = y_coord(iota((256, 256), 0), py)
    yy_t = iota((256, 256), 0) & 15
    cy_t = y_coord(iota((256, 256), 1), py)
    for m in range(2):
        entry = cols[m]
        at = jnp.where(entry >= 0, 8 * (jnp.maximum(entry, 0) & 15) - 4, -4 * FAR)
        sel[m] = one(cy == yy + at)
        sel_t[m] = one(cy_t == yy_t + at)
        listed[8 * m : 8 * m + 8, :] = jnp.full((8, 128), entry, jnp.int32)
    bulk.wait()


def call(kernel, outs, ins, scratch=(), name=None, aliases=None, limit=8 * 2**20):
    return pl.pallas_call(
        kernel,
        out_shape=[jax.ShapeDtypeStruct(s, t) for s, t in outs],
        in_specs=ins,
        out_specs=[VMEM] * len(outs),
        scratch_shapes=scratch,
        name=name,
        compiler_params=pltpu.CompilerParams(vmem_limit_bytes=limit),
        input_output_aliases=aliases or {},
        cost_estimate=pl.CostEstimate(flops=10**6, bytes_accessed=10**6, transcendentals=0),
    )


def swaps(axis, first):
    size = lax.axis_size(axis)
    lows = range(first, size - 1, 2)
    return [(i, i + 1) for i in lows] + [(i + 1, i) for i in lows]


def exchange(a, b, axis):
    return lax.ppermute(a, axis, swaps(axis, 0)), lax.ppermute(b, axis, swaps(axis, 1))


def on_device(
    state, load_vector, active, stiff_band, mass_band, eig_basis, eig_values, cut_cols, cut_inverse
):
    st, ld, active, stiff, mass, basis, values, cols_in, inverse = (
        pltpu.with_memory_space_constraint(x, pltpu.HBM)
        for x in (
            state.reshape(256, 128),
            load_vector.reshape(256, 128),
            active,
            stiff_band,
            mass_band,
            eig_basis,
            eig_values,
            cut_cols.reshape(2),
            cut_inverse.reshape(2, PATCH, 256, 256),
        )
    )
    dma = pltpu.SemaphoreType.DMA
    s, l, ac, ya, yb = call(
        pack_y_kernel,
        [((256, 128), f32), ((256, 128), f32), ((32, 128), f32), ((8, 640), f32), ((8, 640), f32)],
        [ANY] * 3,
        [
            pltpu.VMEM((256, 128), f32),
            pltpu.VMEM((256, 128), bf16),
            pltpu.VMEM((32, 128), jnp.int32),
            pltpu.VMEM((256, 128), f32),
            dma((3,)),
        ],
        name="pack_y",
        limit=8 * 2**20,
    )(st, ld, active)
    ys = exchange(ya, yb, "gy")
    sq = ((256, 256), bf16)
    *mats, inv0, listed = call(
        build_kernel,
        [
            ((256, 512), bf16), ((256, 512), bf16), ((64, 256), bf16), ((64, 256), bf16),
            sq, sq, sq, sq,
            sq, ((128, 256), bf16), ((128, 256), bf16),
            ((256, 256), f32), ((2, 256, 256), bf16), ((2, 256, 256), bf16),
            ((16, 128), bf16), ((16, 128), bf16), ((128, 16), bf16), ((128, 16), bf16),
            ((PATCH, 256, 256), bf16), ((16, 128), jnp.int32),
        ],
        [VMEM] + [ANY] * 6,
        [
            pltpu.SMEM((3, 5), f32),
            pltpu.SMEM((3, 5), f32),
            pltpu.VMEM((3, 16, 16), f32),
            pltpu.VMEM((3, 16), f32),
            pltpu.SMEM((2,), jnp.int32),
            dma((6,)),
        ],
        name="build",
    )(ac, stiff, mass, basis, values, cols_in, inverse)
    yh, yl, lh, ll, ayh, ayl, ath, atl, khl, kth, ktl, dinv, *cutters = mats
    sw, lw, aw, xa, xb = call(
        pack_x_kernel,
        [((256, 256), f32), ((256, 256), f32), ((32, 256), f32), ((120, 128), f32), ((120, 128), f32)],
        [VMEM] * (4 + len(ys)),
        name="pack_x",
    )(lh, s, l, ac, *ys)
    inner_outs = [
        ((256, 512), bf16), ((256, 512), bf16),
        ((320, 256), bf16), ((320, 256), bf16), ((192, 256), bf16), ((192, 256), bf16),
        ((192, 256), f32), ((PATCH, 256, 256), bf16),
    ]
    inner_args = (sw, lw, aw, yh, yl, lh, ll, ayh, ayl, khl, kth, ktl, dinv, listed, inverse)
    xs = exchange(xa, xb, "gx")
    syh, syl, rh, rl, ryh, ryl, tin, inv1 = call(
        inner_kernel, inner_outs, [VMEM] * 14 + [ANY], [dma], name="inner"
    )(*inner_args)
    first, last, cut, xa, xb = call(
        edge_kernel,
        [
            ((96, 256), f32), ((96, 256), f32), ((320, 256), f32),
            ((48, 128), f32), ((48, 128), f32),
        ],
        [VMEM] * (29 + len(xs)),
        [pltpu.VMEM((320, 256), bf16), pltpu.VMEM((320, 256), bf16)],
        name="edge",
    )(
        lw, aw, syh, syl, rh, rl, ryh, ryl, inv0, inv1, listed,
        yh, yl, lh, ll, ayh, ayl, ath, atl, khl, kth, ktl, dinv, *cutters, *xs,
    )
    xs = exchange(xa, xb, "gx")
    core, side = call(
        spread_kernel,
        [((256, 128), f32), ((16, 256), f32)],
        [VMEM] * 17,
        [pltpu.VMEM((320, 256), f32)],
        name="spread",
    )(listed, first, last, tin, cut, ath, atl, rh, rl, inv0, inv1, *cutters)
    ya, yb = call(
        join_x_kernel, [((8, 256), f32), ((8, 256), f32)], [VMEM] * (1 + len(xs)), name="join_x"
    )(side, *xs)
    ys = exchange(ya, yb, "gy")
    (out,) = call(finish_kernel, [((256, 128), f32)], [VMEM] * 7, name="finish")(
        core, s, ac, *xs, *ys
    )
    return out.reshape(8, 32, 128)


def solution(mesh):
    placed = (
        P(None, "gx", "gy"),
        P(None, "gx", "gy"),
        P("gx", "gy"),
        P(),
        P(),
        P(),
        P(),
        P("gx", "gy", None),
        P("gx", "gy", None, None, None, None),
    )
    return jax.shard_map(
        on_device, mesh=mesh, in_specs=placed, out_specs=P(None, "gx", "gy"), check_vma=False
    )
```
